128 devices in a mesh: dom: 8 (over z, core), bulk: 16 (over x, y).
Axes of the slice: x: 4, y: 4, z: 4, core: 2. Of those that a mesh axis runs over, the one named last changes fastest.
Arguments:
- node_patch: int32 [2097152], P(('dom', 'bulk')), may hold values from 0 to 39999, as said below
- node_span: int32 [2097152], P(('dom', 'bulk')), may hold values from 0 to 15
- start_grid: int32 [2, 2097152], P(None, ('dom', 'bulk')), may hold values from 0 to 15
- target: float32 [3, 2097152], P(None, ('dom', 'bulk')), may hold values from -0.1 to 1.1
- net: float32 [40000, 1024], P('bulk'), as said below
Outputs:
- placed: float32 [9, 2097152], P(None, ('dom', 'bulk'))
The draws below stay inside these ranges and needn't reach their ends.
Inputs may be any that keep to these rules, and one draw needn't show every extreme that they name: In each partition's block of 16384 nodes (block k of the array, dom slowest), no owner node_patch // 2500 is named by more than 2560 nodes, and one owner is named by exactly 2560; that owner is the same for all blocks of one index of dom. `net`: component 3 (the weight) of every control point is positive.
All inputs are finite; a program needn't handle non-finite values.
Results may differ from the reference program's by a relative error of at most 0.0003.
Values sent between devices are 32-bit elements; how exact they have to be, the bound alone decides.
A program may use at most 128 MiB of HBM per device.

```python
import jax
import jax.numpy as jnp
from jax import lax

NODE_DEV = 16384
PATCH_DEV = 2500
SPANS = 16
LEVELS = 16
ITERS = 4
CAP = 2560
OWNERS = 16
DOMS = 8
PATCHES = 40000
NODES = 2097152


def draw_node_patch(key, part):
    blocks = NODES // NODE_DEV
    slots = OWNERS * CAP
    busy_key = jax.random.fold_in(key, 11)
    busy = jax.random.randint(busy_key, (DOMS,), 0, OWNERS)
    block_busy = jnp.repeat(busy, blocks // DOMS)

    def one_block(index, chosen):
        block_key = jax.random.fold_in(key, 1000 + index)
        ranks = jax.random.permutation(jax.random.fold_in(block_key, 1), slots)
        slot_owner = jnp.arange(slots) // CAP
        scores = ranks + (slot_owner != chosen).astype(jnp.int32) * slots
        order = jnp.argsort(scores, stable=True)[:NODE_DEV]
        owner = (order // CAP).astype(jnp.int32)
        owner = jax.random.permutation(jax.random.fold_in(block_key, 2), owner)
        local = jax.random.randint(jax.random.fold_in(block_key, 3), (NODE_DEV,), 0, PATCH_DEV)
        return (owner * PATCH_DEV + local).astype(jnp.int32)
    result = jax.vmap(one_block)(jnp.arange(blocks), block_busy)
    return result.reshape(NODES)


def draw_net(key, part):
    shape = (PATCHES, SPANS, 4, 4)
    first = jnp.arange(4, dtype=jnp.float32)[None, None, :, None] / 3.0
    second = jnp.arange(4, dtype=jnp.float32)[None, None, None, :] / 3.0
    rational_weight = jnp.exp(jax.random.uniform(jax.random.fold_in(key, 1), shape, jnp.float32, jnp.log(0.7), jnp.log(1.4)))
    coord_x = first + jax.random.uniform(jax.random.fold_in(key, 2), shape, jnp.float32, -0.1, 0.1)
    coord_y = second + jax.random.uniform(jax.random.fold_in(key, 3), shape, jnp.float32, -0.1, 0.1)
    height = jnp.clip(0.3 * jax.random.normal(jax.random.fold_in(key, 4), shape, jnp.float32), -1.0, 1.0)
    stacked = jnp.stack([rational_weight * coord_x, rational_weight * coord_y, rational_weight * height, rational_weight], axis=2)
    return stacked.reshape(PATCHES, 1024).astype(jnp.float32)


def plant(array, key, least, high):
    longest = array.shape.index(max(array.shape))
    spots = []
    for shift in (0, 1):
        where = [jax.random.randint(jax.random.fold_in(key, axis), (), 0, length) for axis, length in enumerate(array.shape)]
        where[longest] = (where[longest] + shift) % array.shape[longest]
        spots.append(tuple(where))
    return array.at[spots[0]].set(least).at[spots[1]].set(high)


def block_levels(own_key, dims, pieces, smallest, high):
    level, own = 1.0, jax.random.fold_in(own_key, 6)
    for dim, parts in pieces:
        steps = jnp.exp(jax.random.uniform(jax.random.fold_in(own, dim), (parts,), jnp.float32, smallest / len(pieces), high / len(pieces)))
        level = level * jnp.repeat(steps, dims[dim] // parts).reshape([-1 if axis == dim else 1 for axis in range(len(dims))])
    return level


def setup_inputs(seed: int = 0) -> dict:
    keys = jax.random.split(jax.random.key(seed), 6)
    return {
        "node_patch": draw_node_patch(jax.random.fold_in(keys[5], 71), 0),
        "node_span": plant(jax.random.randint(keys[1], (NODES,), 0, SPANS), jax.random.fold_in(keys[1], 1), 0, SPANS - 1).astype(jnp.int32),
        "start_grid": plant(jax.random.randint(keys[2], (2, NODES), 0, LEVELS), jax.random.fold_in(keys[2], 1), 0, LEVELS - 1).astype(jnp.int32),
        "target": jnp.clip(-0.1 + 1.2 * jax.random.uniform(keys[3], (3, NODES), jnp.float32) ** block_levels(keys[3], (3, NODES), ((1, 128),), -0.2, 0.2), -0.1, 1.1),
        "net": draw_net(jax.random.fold_in(keys[5], 71), 0),
    }


damping = 0.1


def bernstein(param):
    other = 1.0 - param
    value = jnp.stack([other * other * other, 3.0 * param * other * other, 3.0 * param * param * other, param * param * param])
    slope = jnp.stack([-3.0 * other * other, 3.0 * other * other - 6.0 * param * other, 6.0 * param * other - 3.0 * param * param, 3.0 * param * param])
    return value, slope


def surface(control, upar, vpar):
    base_u, slope_u = bernstein(upar)
    basis_along_vdir, slope_vdir = bernstein(vpar)
    mixed_partial = jnp.sum(base_u[None, :, None, :] * control, axis=1)
    mixed_partial_udir = jnp.sum(slope_u[None, :, None, :] * control, axis=1)
    homogeneous_point = jnp.sum(basis_along_vdir[None] * mixed_partial, axis=1)
    homogeneous_udiff = jnp.sum(basis_along_vdir[None] * mixed_partial_udir, axis=1)
    homogeneous_vdiff = jnp.sum(slope_vdir[None] * mixed_partial, axis=1)
    rational_weight = homogeneous_point[3]
    surface_point = homogeneous_point[:3] / rational_weight
    tangent_udir = (homogeneous_udiff[:3] - surface_point * homogeneous_udiff[3]) / rational_weight
    tangent_vdir = (homogeneous_vdiff[:3] - surface_point * homogeneous_vdiff[3]) / rational_weight
    return surface_point, tangent_udir, tangent_vdir


def project(coeffs, goal, start):
    control = coeffs.reshape(4, 4, 4, -1)
    upar = start[0]
    vpar = start[1]
    for step in range(ITERS):
        surface_point, tangent_udir, tangent_vdir = surface(control, upar, vpar)
        miss = surface_point - goal
        grad_u = jnp.sum(tangent_udir * miss, axis=0)
        grad_v = jnp.sum(tangent_vdir * miss, axis=0)
        h_uu = jnp.sum(tangent_udir * tangent_udir, axis=0) + damping
        h_vv = jnp.sum(tangent_vdir * tangent_vdir, axis=0) + damping
        h_uv = jnp.sum(tangent_udir * tangent_vdir, axis=0)
        determ = h_uu * h_vv - h_uv * h_uv
        upar = jnp.clip(upar - (h_vv * grad_u - h_uv * grad_v) / determ, 0.0, 1.0)
        vpar = jnp.clip(vpar - (h_uu * grad_v - h_uv * grad_u) / determ, 0.0, 1.0)
    surface_point, tangent_udir, tangent_vdir = surface(control, upar, vpar)
    return jnp.concatenate([surface_point, tangent_udir, tangent_vdir], axis=0)


def reference(node_patch, node_span, start_grid, target, net):
    all_rows = net.reshape(-1, 64)
    row_index = (node_patch * SPANS + node_span).astype(jnp.int32)
    blocks = NODES // NODE_DEV

    def one_block(packed):
        rows, levels, goal = packed
        coeffs = all_rows[rows].T
        start = (levels.astype(jnp.float32) + 0.5) / LEVELS
        return project(coeffs, goal, start)

    result = lax.map(one_block, (row_index.reshape(blocks, NODE_DEV),
                                 start_grid.reshape(2, blocks, NODE_DEV).transpose(1, 0, 2),
                                 target.reshape(3, blocks, NODE_DEV).transpose(1, 0, 2)))
    return result.transpose(1, 0, 2).reshape(9, NODES)
```

```python
import functools

import jax
import jax.numpy as jnp
import numpy as np
from jax import lax
from jax.experimental import pallas as pl
from jax.experimental.pallas import tpu as pltpu
from jax.sharding import PartitionSpec as P

F32 = jnp.float32
BF16 = jnp.bfloat16
I32 = jnp.int32
MESH = pl.DeviceIdType.MESH

SPANS = 16
LEVELS = 16
ITERS = 4
DAMPING = 0.1
OWNERS = 16
PATCH_DEV = 2500
PITCH = 2504
TILES = 20
GROUPS = OWNERS * TILES
MARGIN = 3
BATCH = 8


def iota(shape, dim):
    return lax.broadcasted_iota(I32, shape, dim)


def split3(x):
    high = x.astype(BF16)
    rest = x - high.astype(F32)
    mid = rest.astype(BF16)
    low = (rest - mid.astype(F32)).astype(BF16)
    return jnp.concatenate([high, mid, low], 0)


def block_permutation(place_ref, j):
    place = jnp.concatenate([place_ref[pl.ds(j, 1), :], place_ref[pl.ds(j + 64, 1), :]], 1)
    return jnp.where(iota((256, 256), 0).astype(F32) == place, 1.0, 0.0).astype(BF16)


def dispatch_kernel(patch_ref, span_ref, start_ref, target_ref, out_ref, place_ref, table_ref,
                    code_ref, values, stage, table_v, table_s, sem):
    patch = patch_ref[...]
    span = span_ref[...]
    owner = ((patch.astype(F32) + 0.5) * (1.0 / PATCH_DEV)).astype(I32)
    local = patch - owner * PATCH_DEV
    code_ref[...] = (((span >> 1) * PITCH + local) * 2 + (span & 1)).astype(F32)
    upper = (iota((128, 128), 0) < iota((128, 128), 1)).astype(F32)
    upper = jnp.concatenate([upper, jnp.ones((128, 128), F32)], 1).astype(BF16)
    lower = (iota((64, 64), 0) > iota((64, 64), 1)).astype(F32).astype(BF16)
    lane = iota((64, 128), 1)
    begin = jnp.zeros((64, 128), F32)
    place = jnp.zeros((128, 128), F32)
    table = jnp.zeros((64, 128), I32)
    for o in range(OWNERS):
        mine = (owner == o).astype(F32)
        both = jnp.dot(mine.astype(BF16), upper, preferred_element_type=F32)
        earlier, total = both[:, :128], both[:, 128:]
        count = total[:64] + total[64:]
        base = jnp.dot(lower, count.astype(BF16), preferred_element_type=F32).astype(I32)
        place += mine * jnp.concatenate([earlier[:64] + begin, earlier[64:] + total[:64] + begin], 0)
        first = begin.astype(I32)
        offset = base & 127
        columns = ((offset - first) & 255, offset, base >> 7, offset + count.astype(I32),
                   first, (first - offset) & 255)
        for k, column in enumerate(columns):
            table = jnp.where(lane == k * OWNERS + o, column, table)
        begin = begin + count
    place_ref[...] = place
    table_v[...] = table
    table_ref[...] = table
    copy = pltpu.make_async_copy(table_v, table_s, sem)
    copy.start()
    values[0:3, :] = target_ref[...]
    values[3:5, :] = (start_ref[...].astype(F32) + 0.5) * (1.0 / LEVELS)
    values[5:8, :] = jnp.zeros((3, values.shape[1]), F32)
    stage[...] = jnp.zeros_like(stage)
    copy.wait()
    row = iota((8, 128), 0)
    lane = iota((8, 128), 1)

    def body(j, current):
        halves = []
        for h in range(2):
            r = j + 64 * h
            x = values[:, pl.ds(pl.multiple_of(r * 128, 128), 128)]
            halves.append(jnp.where(row == 5, code_ref[pl.ds(r, 8, stride=0), :], x))
        x = split3(jnp.concatenate(halves, 1))
        y = lax.dot_general(x, block_permutation(place_ref, j), (((1,), (1,)), ((), ())),
                            preferred_element_type=F32)
        y = y[0:8] + y[8:16] + y[16:24]
        following = []
        for o in range(OWNERS):
            rolled = pltpu.roll(y, table_s[j, o], axis=1)
            left, right = rolled[:, :128], rolled[:, 128:]
            offset, tile, end = table_s[j, 16 + o], table_s[j, 32 + o], table_s[j, 48 + o]
            merged = jnp.where(lane >= offset, left, current[o])
            at = pl.multiple_of((o * (TILES + MARGIN) + tile) * 8, 8)
            stage[pl.ds(at, 8), :] = merged
            stage[pl.ds(at + 8, 8), :] = right
            stage[pl.ds(at + 16, 8), :] = left
            following.append(jnp.where(end < 128, merged, jnp.where(end < 256, right, left)))
        return tuple(following)

    lax.fori_loop(0, 64, body, tuple(jnp.zeros((8, 128), F32) for _ in range(OWNERS)))
    for o in range(OWNERS):
        out_ref[o] = stage[pl.ds(o * (TILES + MARGIN) * 8, TILES * 8), :]


def dispatch(patch, span, start, target):
    vmem = pl.BlockSpec(memory_space=pltpu.VMEM)
    return pl.pallas_call(
        dispatch_kernel,
        out_shape=[
            jax.ShapeDtypeStruct((OWNERS, TILES * 8, 128), F32),
            jax.ShapeDtypeStruct((128, 128), F32),
            jax.ShapeDtypeStruct((64, 128), I32),
        ],
        in_specs=[vmem] * 4,
        out_specs=[vmem] * 3,
        scratch_shapes=[
            pltpu.VMEM((128, 128), F32),
            pltpu.VMEM((8, 16384), F32),
            pltpu.VMEM((OWNERS * (TILES + MARGIN) * 8, 128), F32),
            pltpu.VMEM((64, 128), I32),
            pltpu.SMEM((64, 128), I32),
            pltpu.SemaphoreType.DMA,
        ],
        compiler_params=pltpu.CompilerParams(vmem_limit_bytes=32 << 20),
        name="dispatch",
    )(patch.reshape(128, 128), span.reshape(128, 128), start, target)


def exchange_kernel(count, *refs):
    sources, targets = refs[:count], refs[count:2 * count]
    send, recv, own = refs[2 * count:]
    me = lax.axis_index("bulk")
    barrier = pltpu.get_barrier_semaphore()
    for k in range(1, OWNERS):
        peer = lax.rem(me + k, OWNERS)
        pl.semaphore_signal(barrier, inc=1, device_id={"bulk": peer}, device_id_type=MESH)
    local = [pltpu.make_async_copy(s.at[me], t.at[me], own.at[i])
             for i, (s, t) in enumerate(zip(sources, targets))]
    for copy in local:
        copy.start()
    pl.semaphore_wait(barrier, OWNERS - 1)

    def copies(k, dst):
        peer = lax.rem(me + k, OWNERS)
        return [
            pltpu.make_async_remote_copy(
                src_ref=s.at[peer], dst_ref=t.at[dst],
                send_sem=send.at[i, k], recv_sem=recv.at[i, k],
                device_id={"bulk": peer}, device_id_type=MESH,
            )
            for i, (s, t) in enumerate(zip(sources, targets))
        ]

    for k in range(1, OWNERS):
        for copy in copies(k, me):
            copy.start()
    for copy in local:
        copy.wait()
    for k in range(1, OWNERS):
        for copy in copies(k, lax.rem(me + OWNERS - k, OWNERS)):
            copy.wait()


def exchange(arrays, collective_id):
    count = len(arrays)
    hbm = pl.BlockSpec(memory_space=pl.ANY)
    return pl.pallas_call(
        functools.partial(exchange_kernel, count),
        out_shape=[jax.ShapeDtypeStruct(a.shape, a.dtype) for a in arrays],
        in_specs=[hbm] * count,
        out_specs=[hbm] * count,
        scratch_shapes=[
            pltpu.SemaphoreType.DMA((count, OWNERS)),
            pltpu.SemaphoreType.DMA((count, OWNERS)),
            pltpu.SemaphoreType.DMA((count,)),
        ],
        compiler_params=pltpu.CompilerParams(collective_id=collective_id, has_side_effects=True),
        name="exchange%d" % collective_id,
    )(*arrays)


TO_POWERS = np.array([[1, 0, 0, 0], [-3, 3, 0, 0], [3, -6, 3, 0], [-1, 3, -3, 1]], np.float32)


def power_matrix():
    one = np.kron(np.eye(4, dtype=np.float32), np.kron(TO_POWERS, TO_POWERS))
    pair = np.kron(np.eye(2, dtype=np.float32), one)
    return np.concatenate([pair, pair], 1)


def value_slope(a, t):
    b2 = a[3] * t + a[2]
    b1 = b2 * t + a[1]
    return b1 * t + a[0], (a[3] * t + b2) * t + b1


def value_only(a, t):
    return ((a[3] * t + a[2]) * t + a[1]) * t + a[0]


def surface(load, u, v):
    point, along_u, along_v = [], [], []
    for c in range(4):
        values, slopes = [], []
        for j in range(4):
            value, slope = value_slope([load(c * 16 + i * 4 + j) for i in range(4)], u)
            values.append(value)
            slopes.append(slope)
        h, hv = value_slope(values, v)
        point.append(h)
        along_u.append(value_only(slopes, v))
        along_v.append(hv)
    inverse = 1.0 / point[3]
    p = [point[c] * inverse for c in range(3)]
    su = [(along_u[c] - p[c] * along_u[3]) * inverse for c in range(3)]
    sv = [(along_v[c] - p[c] * along_v[3]) * inverse for c in range(3)]
    return p, su, sv


def dot3(a, b):
    return a[0] * b[0] + a[1] * b[1] + a[2] * b[2]


def project(load, goal, u, v):
    for _ in range(ITERS):
        p, su, sv = surface(load, u, v)
        miss = [p[c] - goal[c] for c in range(3)]
        gu, gv = dot3(su, miss), dot3(sv, miss)
        a, d, b = dot3(su, su) + DAMPING, dot3(sv, sv) + DAMPING, dot3(su, sv)
        inverse = 1.0 / (a * d - b * b)
        u, v = (jnp.clip(u - (d * gu - b * gv) * inverse, 0.0, 1.0),
                jnp.clip(v - (a * gv - b * gu) * inverse, 0.0, 1.0))
    return surface(load, u, v)


def project_kernel(recv_ref, net_hbm, powers_ref, main_ref, last_ref,
                   net, index_v, odd, index_s, rows, control, last, sem):
    loads = [
        pltpu.make_async_copy(net_hbm.at[:, pl.ds(k * 128, 128)],
                              net.at[pl.ds(k * PITCH, PATCH_DEV), :], sem.at[k])
        for k in range(8)
    ]
    for copy in loads:
        copy.start()

    def prepare(b, carry):
        code = recv_ref[pl.ds(b * 64 + 5, 8, stride=8), :].astype(I32)
        index_v[pl.ds(b * 8, 8), :] = code >> 1
        odd[pl.ds(b * 8, 8), :] = code & 1
        return carry

    lax.fori_loop(0, GROUPS // BATCH, prepare, 0)
    copy = pltpu.make_async_copy(index_v, index_s, sem.at[8])
    copy.start()
    for each in loads:
        each.wait()
    copy.wait()

    def body(b, carry):
        for g in range(BATCH):
            for t in range(16):
                parts = [net[pl.ds(index_s[b * 8 + g, t * 8 + s], 1), :] for s in range(8)]
                rows[pl.ds(g * 128 + t * 8, 8), :] = jnp.concatenate(parts, 0)
        for h in range(4):
            x = rows[pl.ds(h * 256, 256), :]
            high = x.astype(BF16)
            low = (x - high.astype(F32)).astype(BF16)
            flat = lax.dot_general(powers_ref[...], jnp.concatenate([high, low], 1),
                                   (((1,), (1,)), ((), ())), preferred_element_type=F32)
            for q in range(2):
                which = odd[pl.ds(b * 8 + h * 2 + q, 1), :]
                part = flat[:, q * 128:(q + 1) * 128]
                control[pl.ds((h * 2 + q) * 64, 64), :] = jnp.where(which == 1, part[64:], part[:64])

        def load(k):
            return control[pl.ds(k, 8, stride=64), :]

        def value(k):
            return recv_ref[pl.ds(b * 64 + k, 8, stride=8), :]

        p, su, sv = project(load, [value(0), value(1), value(2)], value(3), value(4))
        for k, x in enumerate((p + su + sv)[:8]):
            main_ref[pl.ds(b * 64 + k, 8, stride=8), :] = x
        last[pl.ds(b * 8, 8), :] = sv[2]
        return carry

    lax.fori_loop(0, GROUPS // BATCH, body, 0)
    for o in range(OWNERS):
        last_ref[o, 0:TILES, :] = last[pl.ds(o * TILES, TILES), :]
        last_ref[o, TILES:24, :] = jnp.zeros((24 - TILES, 128), F32)


def place_nodes(received, net):
    vmem = pl.BlockSpec(memory_space=pltpu.VMEM)
    return pl.pallas_call(
        project_kernel,
        out_shape=[
            jax.ShapeDtypeStruct((GROUPS * 8, 128), F32),
            jax.ShapeDtypeStruct((OWNERS, 24, 128), F32),
        ],
        in_specs=[vmem, pl.BlockSpec(memory_space=pl.ANY), vmem],
        out_specs=[vmem] * 2,
        scratch_shapes=[
            pltpu.VMEM((8 * PITCH, 128), F32),
            pltpu.VMEM((GROUPS, 128), I32),
            pltpu.VMEM((GROUPS, 128), I32),
            pltpu.SMEM((GROUPS, 128), I32),
            pltpu.VMEM((BATCH * 128, 128), F32),
            pltpu.VMEM((BATCH * 64, 128), F32),
            pltpu.VMEM((GROUPS, 128), F32),
            pltpu.SemaphoreType.DMA((9,)),
        ],
        compiler_params=pltpu.CompilerParams(vmem_limit_bytes=48 << 20),
        name="project",
    )(received.reshape(GROUPS * 8, 128), net, jnp.asarray(power_matrix(), BF16))


def collect_kernel(main_hbm, last_hbm, place_ref, table_hbm, out_ref, main, last, table_s, sem):
    copies = [
        pltpu.make_async_copy(main_hbm, main.at[pl.ds(0, GROUPS * 8), :], sem.at[0]),
        pltpu.make_async_copy(last_hbm, last.at[pl.ds(0, OWNERS * 24), :], sem.at[1]),
        pltpu.make_async_copy(table_hbm, table_s, sem.at[2]),
    ]
    for copy in copies:
        copy.start()
    main[pl.ds(GROUPS * 8, 24), :] = jnp.zeros((24, 128), F32)
    for copy in copies:
        copy.wait()
    lane = iota((8, 128), 1)

    def body(j, carry):
        acc = [jnp.zeros((8, 128), F32) for _ in range(4)]
        for o in range(OWNERS):
            offset, tile = table_s[j, 16 + o], table_s[j, 32 + o]
            first, shift = table_s[j, 64 + o], table_s[j, 80 + o]
            keep, low, high = lane >= offset, lane >= first, lane >= first - 128
            at = pl.multiple_of((o * TILES + tile) * 8, 8)
            row = o * 24 + tile
            windows = (
                [main[pl.ds(at + 8 * i, 8), :] for i in range(3)],
                [last[pl.ds(row + i, 8, stride=0), :] for i in range(3)],
            )
            for i, (w0, w1, w2) in enumerate(windows):
                x = jnp.concatenate([jnp.where(keep, w0, w2), w1], 1)
                x = pltpu.roll(x, shift, axis=1)
                acc[2 * i] = jnp.where(low, x[:, :128], acc[2 * i])
                acc[2 * i + 1] = jnp.where(high, x[:, 128:], acc[2 * i + 1])
        x = jnp.concatenate([jnp.concatenate(acc[:2], 1), jnp.concatenate(acc[2:], 1)], 0)
        y = jnp.dot(split3(x), block_permutation(place_ref, j), preferred_element_type=F32)
        y = y[0:16] + y[16:32] + y[32:48]
        for h in range(2):
            at = pl.multiple_of((j + 64 * h) * 128, 128)
            out_ref[:, pl.ds(at, 128)] = y[0:9, h * 128:(h + 1) * 128]
        return carry

    lax.fori_loop(0, 64, body, 0)


def collect(main, last, place, table):
    vmem = pl.BlockSpec(memory_space=pltpu.VMEM)
    hbm = pl.BlockSpec(memory_space=pl.ANY)
    return pl.pallas_call(
        collect_kernel,
        out_shape=jax.ShapeDtypeStruct((9, 16384), F32),
        in_specs=[hbm, hbm, vmem, hbm],
        out_specs=vmem,
        scratch_shapes=[
            pltpu.VMEM((GROUPS * 8 + 24, 128), F32),
            pltpu.VMEM((OWNERS * 24, 128), F32),
            pltpu.SMEM((64, 128), I32),
            pltpu.SemaphoreType.DMA((3,)),
        ],
        compiler_params=pltpu.CompilerParams(vmem_limit_bytes=32 << 20),
        name="collect",
    )(main.reshape(GROUPS * 8, 128), last.reshape(OWNERS * 24, 128), place, table)


def body(node_patch, node_span, start_grid, target, net):
    outgoing, place, table = dispatch(node_patch, node_span, start_grid, target)
    (received,) = exchange([outgoing], 1)
    main, last = place_nodes(received, net)
    main, last = exchange([main.reshape(OWNERS, TILES * 8, 128), last], 2)
    return collect(main, last, place, table)


def solution(mesh):
    return jax.shard_map(
        body,
        mesh=mesh,
        in_specs=(
            P(("dom", "bulk")),
            P(("dom", "bulk")),
            P(None, ("dom", "bulk")),
            P(None, ("dom", "bulk")),
            P("bulk", None),
        ),
        out_specs=P(None, ("dom", "bulk")),
        check_vma=False,
    )
```

```python
import jax
import jax.numpy as jnp
from jax import lax
from jax.experimental import pallas as pl
from jax.experimental.pallas import tpu as pltpu
from jax.sharding import PartitionSpec as P

F32 = jnp.float32
BF16 = jnp.bfloat16
I32 = jnp.int32
MESH = pl.DeviceIdType.MESH

SPANS = 16
LEVELS = 16
ITERS = 4
DAMPING = 0.1
OWNERS = 16
PATCH_DEV = 2500
PITCH = 2504
TABLE = 8 * PITCH
TILES = 20
GROUPS = OWNERS * TILES
MARGIN = 3
BATCH = 8
SLOT = TILES * 8
PAIR_BATCHES = 2 * TILES // BATCH
BATCHES = GROUPS // BATCH


def iota(shape, dim):
    return lax.broadcasted_iota(I32, shape, dim)


def split3(x):
    high = x.astype(BF16)
    rest = x - high.astype(F32)
    mid = rest.astype(BF16)
    low = (rest - mid.astype(F32)).astype(BF16)
    return jnp.concatenate([high, mid, low], 0)


def block_permutation(place_ref, j):
    place = jnp.concatenate([place_ref[pl.ds(j, 1), :], place_ref[pl.ds(j + 64, 1), :]], 1)
    return jnp.where(iota((256, 256), 0).astype(F32) == place, 1.0, 0.0).astype(BF16)


def dispatch_kernel(patch_ref, span_ref, start_ref, target_ref, out_ref, place_ref, table_ref,
                    code_ref, values, stage, table_v, table_s, sem):
    patch = patch_ref[...]
    span = span_ref[...]
    owner = ((patch.astype(F32) + 0.5) * (1.0 / PATCH_DEV)).astype(I32)
    local = patch - owner * PATCH_DEV
    code_ref[...] = ((span & 1) * TABLE + (span >> 1) * PITCH + local).astype(F32)
    upper = (iota((128, 128), 0) < iota((128, 128), 1)).astype(F32)
    upper = jnp.concatenate([upper, jnp.ones((128, 128), F32)], 1).astype(BF16)
    lower = (iota((64, 64), 0) > iota((64, 64), 1)).astype(F32).astype(BF16)
    lane = iota((64, 128), 1)
    begin = jnp.zeros((64, 128), F32)
    place = jnp.zeros((128, 128), F32)
    table = jnp.zeros((64, 128), I32)
    for o in range(OWNERS):
        mine = (owner == o).astype(F32)
        both = jnp.dot(mine.astype(BF16), upper, preferred_element_type=F32)
        earlier, total = both[:, :128], both[:, 128:]
        count = total[:64] + total[64:]
        base = jnp.dot(lower, count.astype(BF16), preferred_element_type=F32).astype(I32)
        place += mine * jnp.concatenate([earlier[:64] + begin, earlier[64:] + total[:64] + begin], 0)
        first = begin.astype(I32)
        offset = base & 127
        columns = ((offset - first) & 255, offset, base >> 7, offset + count.astype(I32),
                   first, (first - offset) & 255)
        for k, column in enumerate(columns):
            table = jnp.where(lane == k * OWNERS + o, column, table)
        begin = begin + count
    place_ref[...] = place
    table_v[...] = table
    table_ref[...] = table
    copy = pltpu.make_async_copy(table_v, table_s, sem)
    copy.start()
    values[0:3, :] = target_ref[...]
    values[3:5, :] = (start_ref[...].astype(F32) + 0.5) * (1.0 / LEVELS)
    values[5:8, :] = jnp.zeros((3, values.shape[1]), F32)
    stage[...] = jnp.zeros_like(stage)
    copy.wait()
    row = iota((8, 128), 0)
    lane = iota((8, 128), 1)

    def body(j, current):
        halves = []
        for h in range(2):
            r = j + 64 * h
            x = values[:, pl.ds(pl.multiple_of(r * 128, 128), 128)]
            halves.append(jnp.where(row == 5, code_ref[pl.ds(r, 8, stride=0), :], x))
        x = split3(jnp.concatenate(halves, 1))
        y = lax.dot_general(x, block_permutation(place_ref, j), (((1,), (1,)), ((), ())),
                            preferred_element_type=F32)
        y = y[0:8] + y[8:16] + y[16:24]
        following = []
        for o in range(OWNERS):
            rolled = pltpu.roll(y, table_s[j, o], axis=1)
            left, right = rolled[:, :128], rolled[:, 128:]
            offset, tile, end = table_s[j, 16 + o], table_s[j, 32 + o], table_s[j, 48 + o]
            merged = jnp.where(lane >= offset, left, current[o])
            at = pl.multiple_of((o * (TILES + MARGIN) + tile) * 8, 8)
            stage[pl.ds(at, 8), :] = merged
            stage[pl.ds(at + 8, 8), :] = right
            stage[pl.ds(at + 16, 8), :] = left
            following.append(jnp.where(end < 128, merged, jnp.where(end < 256, right, left)))
        return tuple(following)

    lax.fori_loop(0, 64, body, tuple(jnp.zeros((8, 128), F32) for _ in range(OWNERS)))
    for o in range(OWNERS):
        out_ref[o] = stage[pl.ds(o * (TILES + MARGIN) * 8, TILES * 8), :]


def dispatch(patch, span, start, target):
    vmem = pl.BlockSpec(memory_space=pltpu.VMEM)
    return pl.pallas_call(
        dispatch_kernel,
        out_shape=[
            jax.ShapeDtypeStruct((OWNERS, TILES * 8, 128), F32),
            jax.ShapeDtypeStruct((128, 128), F32),
            jax.ShapeDtypeStruct((64, 128), I32),
        ],
        in_specs=[vmem] * 4,
        out_specs=[vmem] * 3,
        scratch_shapes=[
            pltpu.VMEM((128, 128), F32),
            pltpu.VMEM((8, 16384), F32),
            pltpu.VMEM((OWNERS * (TILES + MARGIN) * 8, 128), F32),
            pltpu.VMEM((64, 128), I32),
            pltpu.SMEM((64, 128), I32),
            pltpu.SemaphoreType.DMA,
        ],
        compiler_params=pltpu.CompilerParams(vmem_limit_bytes=32 << 20),
        name="dispatch",
    )(patch.reshape(128, 128), span.reshape(128, 128), start, target)


def centre(c0, c1, c2, c3):
    outer, inner = c0 + c3, c1 + c2
    outer_diff, inner_diff = c3 - c0, c2 - c1
    return (0.125 * outer + 0.375 * inner, 0.75 * (outer_diff + inner_diff),
            1.5 * (outer - inner), outer_diff - 3.0 * inner_diff)


def value_slope(a, t):
    b2 = a[3] * t + a[2]
    b1 = b2 * t + a[1]
    return b1 * t + a[0], (a[3] * t + b2) * t + b1


def value_only(a, t):
    return ((a[3] * t + a[2]) * t + a[1]) * t + a[0]


def surface(load, u, v):
    u, v = u - 0.5, v - 0.5
    point, along_u, along_v = [], [], []
    for c in range(4):
        values, slopes = [], []
        for j in range(4):
            value, slope = value_slope([load(c * 16 + i * 4 + j) for i in range(4)], u)
            values.append(value)
            slopes.append(slope)
        h, hv = value_slope(values, v)
        point.append(h)
        along_u.append(value_only(slopes, v))
        along_v.append(hv)
    inverse = 1.0 / point[3]
    p = [point[c] * inverse for c in range(3)]
    su = [(along_u[c] - p[c] * along_u[3]) * inverse for c in range(3)]
    sv = [(along_v[c] - p[c] * along_v[3]) * inverse for c in range(3)]
    return p, su, sv


def dot3(a, b):
    return a[0] * b[0] + a[1] * b[1] + a[2] * b[2]


def project(load, goal, u, v):
    for _ in range(ITERS):
        p, su, sv = surface(load, u, v)
        miss = [p[c] - goal[c] for c in range(3)]
        gu, gv = dot3(su, miss), dot3(sv, miss)
        a, d, b = dot3(su, su) + DAMPING, dot3(sv, sv) + DAMPING, dot3(su, sv)
        inverse = 1.0 / (a * d - b * b)
        u, v = (jnp.clip(u - (d * gu - b * gv) * inverse, 0.0, 1.0),
                jnp.clip(v - (a * gv - b * gu) * inverse, 0.0, 1.0))
    return surface(load, u, v)


def project_kernel(out_ref, net_hbm, main_ref, last_ref,
                   net, recv, index_v, index_a, index_b, rows_a, rows_b, turned, control_a, control_b,
                   main, last, last_pair,
                   net_sem, index_sem, own, send, arrive, back, home):
    me = lax.axis_index("bulk")
    barrier = pltpu.get_barrier_semaphore()
    for k in range(1, OWNERS):
        peer = lax.rem(me + k, OWNERS)
        pl.semaphore_signal(barrier, inc=1, device_id={"bulk": peer}, device_id_type=MESH)
    def net_copy(k):
        return pltpu.make_async_copy(
            net_hbm.at[:, pl.ds(pl.multiple_of(k * 128, 128), 128)],
            net.at[pl.ds(pl.multiple_of(k * PITCH, 8), PATCH_DEV), :], net_sem.at[k])

    for k in range(8):
        net_copy(k).start()
    first = pltpu.make_async_copy(out_ref.at[me], recv.at[pl.ds(0, SLOT), :], own.at[0])
    first.start()
    last[...] = jnp.zeros_like(last)
    pl.semaphore_wait(barrier, OWNERS - 1)

    def outward(k):
        peer = lax.rem(me + k, OWNERS)
        return pltpu.make_async_remote_copy(
            src_ref=out_ref.at[peer],
            dst_ref=recv.at[pl.ds(pl.multiple_of(k * SLOT, 8), SLOT), :],
            send_sem=send.at[k], recv_sem=arrive.at[k],
            device_id={"bulk": peer}, device_id_type=MESH,
        )

    def homeward(k, owner):
        peer = lax.rem(me + OWNERS - k, OWNERS)
        return [
            pltpu.make_async_remote_copy(
                src_ref=s.at[pl.ds(pl.multiple_of(k * n, 8), n), :],
                dst_ref=t.at[pl.ds(pl.multiple_of(owner * n, 8), n), :],
                send_sem=back.at[i, k], recv_sem=home.at[i, k],
                device_id={"bulk": peer}, device_id_type=MESH,
            )
            for i, (s, t, n) in enumerate(((main, main_ref, SLOT), (last, last_ref, 24)))
        ]

    stay = [
        pltpu.make_async_copy(main.at[pl.ds(0, SLOT), :],
                              main_ref.at[pl.ds(pl.multiple_of(me * SLOT, 8), SLOT), :], own.at[1]),
        pltpu.make_async_copy(last.at[pl.ds(0, 24), :],
                              last_ref.at[pl.ds(pl.multiple_of(me * 24, 8), 24), :], own.at[2]),
    ]

    def start_outward(k, carry):
        outward(k).start()
        return carry

    lax.fori_loop(1, OWNERS, start_outward, 0)

    def swap_halves(k, carry):
        net_copy(k).wait()
        for t in range(PITCH // 8):
            at = pl.multiple_of(k * PITCH + t * 8, 8)
            net[pl.ds(pl.multiple_of(at + TABLE, 8), 8), :] = pltpu.roll(net[pl.ds(at, 8), :], 64, axis=1)
        return carry

    lax.fori_loop(0, 8, swap_halves, 0)
    row, lane = iota((8, 128), 0), iota((8, 128), 1)
    masks = [[(row == s) & (lane < 64), (row == s) & (lane >= 64)] for s in range(8)]

    def prepare(m):
        for i in range(PAIR_BATCHES):
            b = m * PAIR_BATCHES + i
            code = recv[pl.ds(b * 64 + 5, 8, stride=8), :].astype(I32)
            code = jnp.clip(code, 0, 2 * TABLE - 1)
            swapped = jnp.where(code >= TABLE, code - TABLE, code + TABLE)
            index_v[b] = jnp.where((row & 1) == 1, swapped, code)

    def index_copy(b, half):
        return pltpu.make_async_copy(index_v.at[b], (index_a, index_b)[half], index_sem.at[half])

    def gather(index, rows):
        for h in range(4):
            for t in range(16):
                x = None
                for s in range(8):
                    for q in range(2):
                        w = net[pl.ds(index[2 * h + q, t * 8 + s], 8, stride=0), :]
                        x = w if x is None else jnp.where(masks[s][q], w, x)
                rows[pl.ds(h * 128 + t * 8, 8), :] = x

    def to_powers(rows, control):
        for h in range(4):
            turned[pl.ds(h * 128, 128), :] = rows[pl.ds(h * 128, 128), :].T
        for c in range(4):
            along = [
                centre(*[turned[pl.ds(c * 16 + i * 4 + j, 8, stride=64), :] for i in range(4)])
                for j in range(4)
            ]
            for i in range(4):
                for j, x in enumerate(centre(*[along[j][i] for j in range(4)])):
                    control[c * 16 + i * 4 + j] = x

    first.wait()
    outward(1).wait_recv()
    prepare(0)
    for half, (index, rows) in enumerate(((index_a, rows_a), (index_b, rows_b))):
        index_copy(half, half).start()
        index_copy(half, half).wait()
        gather(index, rows)
        index_copy(half + 2, half).start()
    to_powers(rows_a, control_a)

    def batch(b, half):
        index, rows, other, control, following = (
            (index_a, rows_a, rows_b, control_a, control_b),
            (index_b, rows_b, rows_a, control_b, control_a),
        )[half]
        m = lax.div(b, PAIR_BATCHES)
        i = b - m * PAIR_BATCHES
        index_copy(0, half).wait()
        gather(index, rows)
        to_powers(other, following)

        def load(k):
            return control[k]

        def value(k):
            return recv[pl.ds(b * 64 + k, 8, stride=8), :]

        p, su, sv = project(load, [value(0), value(1), value(2)], value(3), value(4))
        for k, x in enumerate((p + su + sv)[:8]):
            main[pl.ds(b * 64 + k, 8, stride=8), :] = x
        last_pair[pl.ds(pl.multiple_of(i * 8, 8), 8), :] = sv[2]

        @pl.when((i == 1) & (m < OWNERS // 2 - 1))
        def _():
            outward(2 * m + 2).wait_recv()
            outward(2 * m + 3).wait_recv()
            prepare(m + 1)

        index_copy(jnp.minimum(b + 4, BATCHES - 1), half).start()

        @pl.when(i == PAIR_BATCHES - 1)
        def _():
            for h in range(2):
                at = pl.multiple_of((2 * m + h) * 24, 8)
                last[pl.ds(at, TILES), :] = last_pair[h * TILES:(h + 1) * TILES, :]

            @pl.when(m == 0)
            def _():
                for copy in stay:
                    copy.start()

            @pl.when(m > 0)
            def _():
                for copy in homeward(2 * m, me):
                    copy.start()

            for copy in homeward(2 * m + 1, me):
                copy.start()

    def two(q, carry):
        batch(2 * q, 0)
        batch(2 * q + 1, 1)
        return carry

    lax.fori_loop(0, BATCHES // 2, two, 0)
    for half in range(2):
        index_copy(0, half).wait()
    for copy in stay:
        copy.wait()

    def finish(k, carry):
        outward(k).wait_send()
        for copy in homeward(k, lax.rem(me + k, OWNERS)):
            copy.wait()
        return carry

    lax.fori_loop(1, OWNERS, finish, 0)


def place_nodes(outgoing, net):
    vmem = pl.BlockSpec(memory_space=pltpu.VMEM)
    dma = pltpu.SemaphoreType.DMA
    return pl.pallas_call(
        project_kernel,
        out_shape=[
            jax.ShapeDtypeStruct((GROUPS * 8 + 24, 128), F32),
            jax.ShapeDtypeStruct((OWNERS * 24, 128), F32),
        ],
        in_specs=[vmem, pl.BlockSpec(memory_space=pl.ANY)],
        out_specs=[vmem] * 2,
        scratch_shapes=[
            pltpu.VMEM((2 * TABLE, 128), F32),
            pltpu.VMEM((GROUPS * 8 + 64, 128), F32),
            pltpu.VMEM((BATCHES, 8, 128), I32),
            pltpu.SMEM((8, 128), I32),
            pltpu.SMEM((8, 128), I32),
            pltpu.VMEM((BATCH * 64, 128), F32),
            pltpu.VMEM((BATCH * 64, 128), F32),
            pltpu.VMEM((BATCH * 64 + 64, 128), F32),
            pltpu.VMEM((64, 8, 128), F32),
            pltpu.VMEM((64, 8, 128), F32),
            pltpu.VMEM((GROUPS * 8 + 64, 128), F32),
            pltpu.VMEM((OWNERS * 24, 128), F32),
            pltpu.VMEM((2 * TILES, 128), F32),
            dma((8,)), dma((2,)), dma((3,)),
            dma((OWNERS,)), dma((OWNERS,)), dma((2, OWNERS)), dma((2, OWNERS)),
        ],
        compiler_params=pltpu.CompilerParams(
            collective_id=1, has_side_effects=True, vmem_limit_bytes=48 << 20),
        name="project",
    )(outgoing, net)


def collect_kernel(main, last, place_ref, table_hbm, out_ref, table_s, sem):
    copy = pltpu.make_async_copy(table_hbm, table_s, sem)
    copy.start()
    copy.wait()
    lane = iota((8, 128), 1)

    def body(j, carry):
        acc = [jnp.zeros((8, 128), F32) for _ in range(4)]
        for o in range(OWNERS):
            offset, tile = table_s[j, 16 + o], table_s[j, 32 + o]
            first, shift = table_s[j, 64 + o], table_s[j, 80 + o]
            keep, low, high = lane >= offset, lane >= first, lane >= first - 128
            at = pl.multiple_of((o * TILES + tile) * 8, 8)
            row = o * 24 + tile
            windows = (
                [main[pl.ds(at + 8 * i, 8), :] for i in range(3)],
                [last[pl.ds(row + i, 8, stride=0), :] for i in range(3)],
            )
            for i, (w0, w1, w2) in enumerate(windows):
                x = jnp.concatenate([jnp.where(keep, w0, w2), w1], 1)
                x = pltpu.roll(x, shift, axis=1)
                acc[2 * i] = jnp.where(low, x[:, :128], acc[2 * i])
                acc[2 * i + 1] = jnp.where(high, x[:, 128:], acc[2 * i + 1])
        x = jnp.concatenate([jnp.concatenate(acc[:2], 1), jnp.concatenate(acc[2:], 1)], 0)
        y = jnp.dot(split3(x), block_permutation(place_ref, j), preferred_element_type=F32)
        y = y[0:16] + y[16:32] + y[32:48]
        for h in range(2):
            at = pl.multiple_of((j + 64 * h) * 128, 128)
            out_ref[:, pl.ds(at, 128)] = y[0:9, h * 128:(h + 1) * 128]
        return carry

    lax.fori_loop(0, 64, body, 0)


def collect(main, last, place, table):
    vmem = pl.BlockSpec(memory_space=pltpu.VMEM)
    hbm = pl.BlockSpec(memory_space=pl.ANY)
    return pl.pallas_call(
        collect_kernel,
        out_shape=jax.ShapeDtypeStruct((9, 16384), F32),
        in_specs=[vmem, vmem, vmem, hbm],
        out_specs=vmem,
        scratch_shapes=[pltpu.SMEM((64, 128), I32), pltpu.SemaphoreType.DMA],
        compiler_params=pltpu.CompilerParams(vmem_limit_bytes=32 << 20),
        name="collect",
    )(main, last, place, table)


def body(node_patch, node_span, start_grid, target, net):
    outgoing, place, table = dispatch(node_patch, node_span, start_grid, target)
    main, last = place_nodes(outgoing, net)
    return collect(main, last, place, table)


def solution(mesh):
    return jax.shard_map(
        body,
        mesh=mesh,
        in_specs=(
            P(("dom", "bulk")),
            P(("dom", "bulk")),
            P(None, ("dom", "bulk")),
            P(None, ("dom", "bulk")),
            P("bulk", None),
        ),
        out_specs=P(None, ("dom", "bulk")),
        check_vma=False,
    )
```

```python
import jax
import jax.numpy as jnp
from jax import lax
from jax.experimental import pallas as pl
from jax.experimental.pallas import tpu as pltpu
from jax.sharding import PartitionSpec as P

F32 = jnp.float32
BF16 = jnp.bfloat16
I32 = jnp.int32
MESH = pl.DeviceIdType.MESH

SPANS = 16
LEVELS = 16
ITERS = 4
DAMPING = 0.1
OWNERS = 16
PATCH_DEV = 2500
PITCH = 2504
TABLE = 8 * PITCH
TILES = 20
GROUPS = OWNERS * TILES
MARGIN = 3
BATCH = 8
TURN = 72
SLOT = TILES * 8
PAIR_BATCHES = 2 * TILES // BATCH
BATCHES = GROUPS // BATCH


def iota(shape, dim):
    return lax.broadcasted_iota(I32, shape, dim)


def split3(x):
    high = x.astype(BF16)
    rest = x - high.astype(F32)
    mid = rest.astype(BF16)
    low = (rest - mid.astype(F32)).astype(BF16)
    return jnp.concatenate([high, mid, low], 0)


def block_permutation(place_ref, j):
    place = jnp.concatenate([place_ref[pl.ds(j, 1), :], place_ref[pl.ds(j + 64, 1), :]], 1)
    return jnp.where(iota((256, 256), 0).astype(F32) == place, 1.0, 0.0).astype(BF16)


def dispatch_kernel(patch_hbm, span_hbm, start_hbm, target_hbm, out_ref, place_ref, table_ref,
                    patch_ref, span_ref, start_ref, code_ref, values, ordered, stage, table_v, table_s, sem):
    copies = [
        pltpu.make_async_copy(patch_hbm, patch_ref, sem.at[0]),
        pltpu.make_async_copy(span_hbm, span_ref, sem.at[1]),
        pltpu.make_async_copy(start_hbm, start_ref, sem.at[2]),
        pltpu.make_async_copy(target_hbm, values.at[pl.ds(0, 3), :], sem.at[3]),
    ]
    for copy in copies:
        copy.start()
    stage[...] = jnp.zeros_like(stage)
    copies[0].wait()
    copies[1].wait()
    patch = patch_ref[...]
    span = span_ref[...]
    owner = ((patch.astype(F32) + 0.5) * (1.0 / PATCH_DEV)).astype(I32)
    local = patch - owner * PATCH_DEV
    code_ref[...] = ((span & 1) * TABLE + (span >> 1) * PITCH + local).astype(F32)
    upper = (iota((128, 128), 0) < iota((128, 128), 1)).astype(F32)
    upper = jnp.concatenate([upper, jnp.ones((128, 128), F32)], 1).astype(BF16)
    lower = (iota((64, 64), 0) > iota((64, 64), 1)).astype(F32).astype(BF16)
    lane = iota((64, 128), 1)
    begin = jnp.zeros((64, 128), F32)
    place = jnp.zeros((128, 128), F32)
    table = jnp.zeros((64, 128), I32)
    for o in range(OWNERS):
        mine = (owner == o).astype(F32)
        both = jnp.dot(mine.astype(BF16), upper, preferred_element_type=F32)
        earlier, total = both[:, :128], both[:, 128:]
        count = total[:64] + total[64:]
        base = jnp.dot(lower, count.astype(BF16), preferred_element_type=F32).astype(I32)
        place += mine * jnp.concatenate([earlier[:64] + begin, earlier[64:] + total[:64] + begin], 0)
        first = begin.astype(I32)
        offset = base & 127
        columns = (offset - first, offset, base >> 7, offset + count.astype(I32), first)
        for k, column in enumerate(columns):
            table = jnp.where(lane == k * OWNERS + o, column, table)
        begin = begin + count
    place_ref[...] = place
    table_v[...] = table
    table_ref[...] = table
    copy = pltpu.make_async_copy(table_v, table_s, sem.at[4])
    copy.start()
    copies[2].wait()
    copies[3].wait()
    values[3:5, :] = (start_ref[...].astype(F32) + 0.5) * (1.0 / LEVELS)
    values[5:8, :] = jnp.zeros((3, values.shape[1]), F32)
    row = iota((8, 128), 0)
    lane = iota((8, 128), 1)

    def order(i, carry):
        for step in range(4):
            j = i * 4 + step
            halves = []
            for h in range(2):
                r = j + 64 * h
                x = values[:, pl.ds(pl.multiple_of(r * 128, 128), 128)]
                halves.append(jnp.where(row == 5, code_ref[pl.ds(r, 8, stride=0), :], x))
            x = split3(jnp.concatenate(halves, 1))
            y = lax.dot_general(x, block_permutation(place_ref, j), (((1,), (1,)), ((), ())),
                                preferred_element_type=F32)
            ordered[j] = y[0:8] + y[8:16] + y[16:24]
        return carry

    lax.fori_loop(0, 16, order, 0)
    copy.wait()

    def append(i, current):
        current = list(current)
        for step in range(2):
            j = i * 2 + step
            y0, y1 = ordered[j, :, 0:128], ordered[j, :, 128:256]
            for o in range(OWNERS):
                move, offset = table_s[j, o], table_s[j, 16 + o]
                tile, end = table_s[j, 32 + o], table_s[j, 48 + o]
                r0 = pltpu.roll(y0, move & 127, axis=1)
                r1 = pltpu.roll(y1, move & 127, axis=1)
                second = jnp.where(lane >= move, r1, r0)
                merged = jnp.where(lane >= offset, jnp.where(lane >= move + 128, r1, r0), current[o])
                at = pl.multiple_of((o * (TILES + MARGIN) + tile) * 8, 8)
                stage[pl.ds(at, 8), :] = merged
                stage[pl.ds(at + 8, 8), :] = second
                stage[pl.ds(at + 16, 8), :] = r1
                current[o] = jnp.where(end < 128, merged, jnp.where(end < 256, second, r1))
        return tuple(current)

    lax.fori_loop(0, 32, append, tuple(jnp.zeros((8, 128), F32) for _ in range(OWNERS)))
    for o in range(OWNERS):
        out_ref[o] = stage[pl.ds(o * (TILES + MARGIN) * 8, TILES * 8), :]


def dispatch(patch, span, start, target):
    vmem = pl.BlockSpec(memory_space=pltpu.VMEM)
    return pl.pallas_call(
        dispatch_kernel,
        out_shape=[
            jax.ShapeDtypeStruct((OWNERS, TILES * 8, 128), F32),
            jax.ShapeDtypeStruct((128, 128), F32),
            jax.ShapeDtypeStruct((64, 128), I32),
        ],
        in_specs=[pl.BlockSpec(memory_space=pl.ANY)] * 4,
        out_specs=[vmem] * 3,
        scratch_shapes=[
            pltpu.VMEM((128, 128), I32),
            pltpu.VMEM((128, 128), I32),
            pltpu.VMEM((2, 16384), I32),
            pltpu.VMEM((128, 128), F32),
            pltpu.VMEM((8, 16384), F32),
            pltpu.VMEM((64, 8, 256), F32),
            pltpu.VMEM((OWNERS * (TILES + MARGIN) * 8, 128), F32),
            pltpu.VMEM((64, 128), I32),
            pltpu.SMEM((64, 128), I32),
            pltpu.SemaphoreType.DMA((5,)),
        ],
        compiler_params=pltpu.CompilerParams(vmem_limit_bytes=62 << 20),
        name="dispatch",
    )(patch.reshape(128, 128), span.reshape(128, 128), start, target)


def centre(c0, c1, c2, c3):
    outer, inner = c0 + c3, c1 + c2
    outer_diff, inner_diff = c3 - c0, c2 - c1
    return (0.125 * outer + 0.375 * inner, 0.75 * (outer_diff + inner_diff),
            1.5 * (outer - inner), outer_diff - 3.0 * inner_diff)


def value_slope(a, t):
    b2 = a[3] * t + a[2]
    b1 = b2 * t + a[1]
    return b1 * t + a[0], (a[3] * t + b2) * t + b1


def value_only(a, t):
    return ((a[3] * t + a[2]) * t + a[1]) * t + a[0]


def surface(load, u, v):
    u, v = u - 0.5, v - 0.5
    point, along_u, along_v = [], [], []
    for c in range(4):
        values, slopes = [], []
        for j in range(4):
            value, slope = value_slope([load(c * 16 + i * 4 + j) for i in range(4)], u)
            values.append(value)
            slopes.append(slope)
        h, hv = value_slope(values, v)
        point.append(h)
        along_u.append(value_only(slopes, v))
        along_v.append(hv)
    inverse = 1.0 / point[3]
    p = [point[c] * inverse for c in range(3)]
    su = [(along_u[c] - p[c] * along_u[3]) * inverse for c in range(3)]
    sv = [(along_v[c] - p[c] * along_v[3]) * inverse for c in range(3)]
    return p, su, sv


def dot3(a, b):
    return a[0] * b[0] + a[1] * b[1] + a[2] * b[2]


def project(load, goal, u, v):
    for _ in range(ITERS):
        p, su, sv = surface(load, u, v)
        miss = [p[c] - goal[c] for c in range(3)]
        gu, gv = dot3(su, miss), dot3(sv, miss)
        a, d, b = dot3(su, su) + DAMPING, dot3(sv, sv) + DAMPING, dot3(su, sv)
        inverse = 1.0 / (a * d - b * b)
        u, v = (jnp.clip(u - (d * gu - b * gv) * inverse, 0.0, 1.0),
                jnp.clip(v - (a * gv - b * gu) * inverse, 0.0, 1.0))
    return surface(load, u, v)


def project_kernel(out_ref, net_hbm, main_ref, last_ref,
                   net, recv, index_v, index_a, index_b, rows_a, rows_b, turned, control_a, control_b,
                   main, last, last_pair,
                   net_sem, index_sem, own, send, arrive, back, home):
    me = lax.axis_index("bulk")
    barrier = pltpu.get_barrier_semaphore()
    for k in range(1, OWNERS):
        peer = lax.rem(me + k, OWNERS)
        pl.semaphore_signal(barrier, inc=1, device_id={"bulk": peer}, device_id_type=MESH)
    def net_copy(k):
        return pltpu.make_async_copy(
            net_hbm.at[:, pl.ds(pl.multiple_of(k * 128, 128), 128)],
            net.at[pl.ds(pl.multiple_of(k * PITCH, 8), PATCH_DEV), :], net_sem.at[k])

    for k in range(8):
        net_copy(k).start()
    first = pltpu.make_async_copy(out_ref.at[me], recv.at[pl.ds(0, SLOT), :], own.at[0])
    first.start()
    last[...] = jnp.zeros_like(last)
    pl.semaphore_wait(barrier, OWNERS - 1)

    def outward(k):
        peer = lax.rem(me + k, OWNERS)
        return pltpu.make_async_remote_copy(
            src_ref=out_ref.at[peer],
            dst_ref=recv.at[pl.ds(pl.multiple_of(k * SLOT, 8), SLOT), :],
            send_sem=send.at[k], recv_sem=arrive.at[k],
            device_id={"bulk": peer}, device_id_type=MESH,
        )

    def homeward(k, owner):
        peer = lax.rem(me + OWNERS - k, OWNERS)
        return [
            pltpu.make_async_remote_copy(
                src_ref=s.at[pl.ds(pl.multiple_of(k * n, 8), n), :],
                dst_ref=t.at[pl.ds(pl.multiple_of(owner * n, 8), n), :],
                send_sem=back.at[i, k], recv_sem=home.at[i, k],
                device_id={"bulk": peer}, device_id_type=MESH,
            )
            for i, (s, t, n) in enumerate(((main, main_ref, SLOT), (last, last_ref, 24)))
        ]

    stay = [
        pltpu.make_async_copy(main.at[pl.ds(0, SLOT), :],
                              main_ref.at[pl.ds(pl.multiple_of(me * SLOT, 8), SLOT), :], own.at[1]),
        pltpu.make_async_copy(last.at[pl.ds(0, 24), :],
                              last_ref.at[pl.ds(pl.multiple_of(me * 24, 8), 24), :], own.at[2]),
    ]

    def start_outward(k, carry):
        outward(k).start()
        return carry

    lax.fori_loop(1, OWNERS, start_outward, 0)

    def swap_halves(k, carry):
        net_copy(k).wait()
        for t in range(PITCH // 8):
            at = pl.multiple_of(k * PITCH + t * 8, 8)
            net[pl.ds(pl.multiple_of(at + TABLE, 8), 8), :] = pltpu.roll(net[pl.ds(at, 8), :], 64, axis=1)
        return carry

    lax.fori_loop(0, 8, swap_halves, 0)
    row, lane = iota((8, 128), 0), iota((8, 128), 1)
    masks = [[(row == s) & (lane < 64), (row == s) & (lane >= 64)] for s in range(8)]

    def prepare(m):
        for i in range(PAIR_BATCHES):
            b = m * PAIR_BATCHES + i
            code = recv[pl.ds(b * 64 + 5, 8, stride=8), :].astype(I32)
            code = jnp.clip(code, 0, 2 * TABLE - 1)
            swapped = jnp.where(code >= TABLE, code - TABLE, code + TABLE)
            index_v[b] = jnp.where((row & 1) == 1, swapped, code)

    def index_copy(b, half):
        return pltpu.make_async_copy(index_v.at[b], (index_a, index_b)[half], index_sem.at[half])

    def gather(index, rows):
        for h in range(4):
            for t in range(16):
                x = None
                for s in range(8):
                    for q in range(2):
                        w = net[pl.ds(index[2 * h + q, t * 8 + s], 8, stride=0), :]
                        x = w if x is None else jnp.where(masks[s][q], w, x)
                rows[pl.ds(h * 128 + t * 8, 8), :] = x

    def to_powers(rows, control):
        for h in range(4):
            both = rows[pl.ds(h * 128, 128), :].T
            turned[pl.ds(2 * h * TURN, 64), :] = both[:64]
            turned[pl.ds((2 * h + 1) * TURN, 64), :] = both[64:]
        for c in range(4):
            along = [
                centre(*[turned[pl.ds(c * 16 + i * 4 + j, 8, stride=TURN), :] for i in range(4)])
                for j in range(4)
            ]
            for i in range(4):
                for j, x in enumerate(centre(*[along[j][i] for j in range(4)])):
                    control[c * 16 + i * 4 + j] = x

    first.wait()
    outward(1).wait_recv()
    prepare(0)
    for half, (index, rows) in enumerate(((index_a, rows_a), (index_b, rows_b))):
        index_copy(half, half).start()
        index_copy(half, half).wait()
        gather(index, rows)
        index_copy(half + 2, half).start()
    to_powers(rows_a, control_a)

    def batch(b, half):
        index, rows, other, control, following = (
            (index_a, rows_a, rows_b, control_a, control_b),
            (index_b, rows_b, rows_a, control_b, control_a),
        )[half]
        m = lax.div(b, PAIR_BATCHES)
        i = b - m * PAIR_BATCHES
        index_copy(0, half).wait()
        gather(index, rows)
        to_powers(other, following)

        def load(k):
            return control[k]

        def value(k):
            return recv[pl.ds(b * 64 + k, 8, stride=8), :]

        p, su, sv = project(load, [value(0), value(1), value(2)], value(3), value(4))
        for k, x in enumerate((p + su + sv)[:8]):
            main[pl.ds(b * 64 + k, 8, stride=8), :] = x
        last_pair[pl.ds(pl.multiple_of(i * 8, 8), 8), :] = sv[2]

        @pl.when((i == 1) & (m < OWNERS // 2 - 1))
        def _():
            outward(2 * m + 2).wait_recv()
            outward(2 * m + 3).wait_recv()
            prepare(m + 1)

        index_copy(jnp.minimum(b + 4, BATCHES - 1), half).start()

        @pl.when(i == PAIR_BATCHES - 1)
        def _():
            for h in range(2):
                at = pl.multiple_of((2 * m + h) * 24, 8)
                last[pl.ds(at, TILES), :] = last_pair[h * TILES:(h + 1) * TILES, :]

            @pl.when(m == 0)
            def _():
                for copy in stay:
                    copy.start()

            @pl.when(m > 0)
            def _():
                for copy in homeward(2 * m, me):
                    copy.start()

            for copy in homeward(2 * m + 1, me):
                copy.start()

    def two(q, carry):
        batch(2 * q, 0)
        batch(2 * q + 1, 1)
        return carry

    lax.fori_loop(0, BATCHES // 2, two, 0)
    for half in range(2):
        index_copy(0, half).wait()
    for copy in stay:
        copy.wait()

    def finish(k, carry):
        outward(k).wait_send()
        for copy in homeward(k, lax.rem(me + k, OWNERS)):
            copy.wait()
        return carry

    lax.fori_loop(1, OWNERS, finish, 0)


def place_nodes(outgoing, net):
    vmem = pl.BlockSpec(memory_space=pltpu.VMEM)
    dma = pltpu.SemaphoreType.DMA
    return pl.pallas_call(
        project_kernel,
        out_shape=[
            jax.ShapeDtypeStruct((GROUPS * 8 + 24, 128), F32),
            jax.ShapeDtypeStruct((OWNERS * 24, 128), F32),
        ],
        in_specs=[vmem, pl.BlockSpec(memory_space=pl.ANY)],
        out_specs=[vmem] * 2,
        scratch_shapes=[
            pltpu.VMEM((2 * TABLE, 128), F32),
            pltpu.VMEM((GROUPS * 8 + 64, 128), F32),
            pltpu.VMEM((BATCHES, 8, 128), I32),
            pltpu.SMEM((8, 128), I32),
            pltpu.SMEM((8, 128), I32),
            pltpu.VMEM((BATCH * 64, 128), F32),
            pltpu.VMEM((BATCH * 64, 128), F32),
            pltpu.VMEM((BATCH * TURN + 64, 128), F32),
            pltpu.VMEM((64, 8, 128), F32),
            pltpu.VMEM((64, 8, 128), F32),
            pltpu.VMEM((GROUPS * 8 + 64, 128), F32),
            pltpu.VMEM((OWNERS * 24, 128), F32),
            pltpu.VMEM((2 * TILES, 128), F32),
            dma((8,)), dma((2,)), dma((3,)),
            dma((OWNERS,)), dma((OWNERS,)), dma((2, OWNERS)), dma((2, OWNERS)),
        ],
        compiler_params=pltpu.CompilerParams(
            collective_id=1, has_side_effects=True, vmem_limit_bytes=48 << 20),
        name="project",
    )(outgoing, net)


def collect_kernel(main, last, place_ref, table_hbm, out_ref, ordered, table_s, sem):
    copy = pltpu.make_async_copy(table_hbm, table_s, sem)
    copy.start()
    copy.wait()
    lane = iota((8, 128), 1)

    def assemble(i, carry):
        for step in range(2):
            j = i * 2 + step
            acc = [jnp.zeros((8, 128), F32) for _ in range(4)]
            for o in range(OWNERS):
                move, offset = table_s[j, o], table_s[j, 16 + o]
                tile, first = table_s[j, 32 + o], table_s[j, 64 + o]
                at = pl.multiple_of((o * TILES + tile) * 8, 8)
                at_last = o * 24 + tile
                keep = lane >= offset
                in_low, in_high = lane >= first, lane >= first - 128
                from_low = lane >= 128 - move
                from_high = (lane >= -move) & (lane < 128 - move)
                windows = (
                    [main[pl.ds(at + 8 * k, 8), :] for k in range(3)],
                    [last[pl.ds(at_last + k, 8, stride=0), :] for k in range(3)],
                )
                for k, (w0, w1, w2) in enumerate(windows):
                    r0 = pltpu.roll(jnp.where(keep, w0, w2), (-move) & 127, axis=1)
                    r1 = pltpu.roll(w1, (-move) & 127, axis=1)
                    acc[2 * k] = jnp.where(in_low, jnp.where(from_low, r1, r0), acc[2 * k])
                    acc[2 * k + 1] = jnp.where(in_high, jnp.where(from_high, r1, r0), acc[2 * k + 1])
            for k in range(2):
                ordered[j, 8 * k:8 * k + 8, 0:128] = acc[2 * k]
                ordered[j, 8 * k:8 * k + 8, 128:256] = acc[2 * k + 1]
        return carry

    lax.fori_loop(0, 32, assemble, 0)

    def spread(i, carry):
        for step in range(4):
            j = i * 4 + step
            y = jnp.dot(split3(ordered[j]), block_permutation(place_ref, j), preferred_element_type=F32)
            y = y[0:16] + y[16:32] + y[32:48]
            for h in range(2):
                at = pl.multiple_of((j + 64 * h) * 128, 128)
                out_ref[:, pl.ds(at, 128)] = y[0:9, h * 128:(h + 1) * 128]
        return carry

    lax.fori_loop(0, 16, spread, 0)


def collect(main, last, place, table):
    vmem = pl.BlockSpec(memory_space=pltpu.VMEM)
    hbm = pl.BlockSpec(memory_space=pl.ANY)
    return pl.pallas_call(
        collect_kernel,
        out_shape=jax.ShapeDtypeStruct((9, 16384), F32),
        in_specs=[vmem, vmem, vmem, hbm],
        out_specs=vmem,
        scratch_shapes=[pltpu.VMEM((64, 16, 256), F32), pltpu.SMEM((64, 128), I32), pltpu.SemaphoreType.DMA],
        compiler_params=pltpu.CompilerParams(vmem_limit_bytes=32 << 20),
        name="collect",
    )(main, last, place, table)


def body(node_patch, node_span, start_grid, target, net):
    outgoing, place, table = dispatch(node_patch, node_span, start_grid, target)
    main, last = place_nodes(outgoing, net)
    return collect(main, last, place, table)


def solution(mesh):
    return jax.shard_map(
        body,
        mesh=mesh,
        in_specs=(
            P(("dom", "bulk")),
            P(("dom", "bulk")),
            P(None, ("dom", "bulk")),
            P(None, ("dom", "bulk")),
            P("bulk", None),
        ),
        out_specs=P(None, ("dom", "bulk")),
        check_vma=False,
    )
```

```python
import jax
import jax.numpy as jnp
from jax import lax
from jax.experimental import pallas as pl
from jax.experimental.pallas import tpu as pltpu
from jax.sharding import PartitionSpec as P

F32 = jnp.float32
BF16 = jnp.bfloat16
I32 = jnp.int32
MESH = pl.DeviceIdType.MESH

SPANS = 16
LEVELS = 16
ITERS = 4
DAMPING = 0.1
OWNERS = 16
PATCH_DEV = 2500
PITCH = 2504
TABLE = 8 * PITCH
TILES = 20
GROUPS = OWNERS * TILES
MARGIN = 3
STEPS = 4
BATCH = 8
TURN = 72
SLOT = TILES * 8
PAIR_BATCHES = 2 * TILES // BATCH
BATCHES = GROUPS // BATCH


def iota(shape, dim):
    return lax.broadcasted_iota(I32, shape, dim)


def split3(x):
    high = x.astype(BF16)
    rest = x - high.astype(F32)
    mid = rest.astype(BF16)
    low = (rest - mid.astype(F32)).astype(BF16)
    return jnp.concatenate([high, mid, low], 0)


def block_permutation(place_ref, j):
    place = jnp.concatenate([place_ref[pl.ds(j, 1), :], place_ref[pl.ds(j + 64, 1), :]], 1)
    return jnp.where(iota((256, 256), 0).astype(F32) == place, 1.0, 0.0).astype(BF16)


def dispatch_kernel(patch_hbm, span_hbm, start_hbm, target_hbm, out_ref, place_ref, table_ref,
                    patch_ref, span_ref, start_ref, code_ref, values, ordered, stage, table_v, table_s, sem):
    copies = [
        pltpu.make_async_copy(patch_hbm, patch_ref, sem.at[0]),
        pltpu.make_async_copy(span_hbm, span_ref, sem.at[1]),
        pltpu.make_async_copy(start_hbm, start_ref, sem.at[2]),
        pltpu.make_async_copy(target_hbm, values.at[pl.ds(0, 3), :], sem.at[3]),
    ]
    for copy in copies:
        copy.start()
    stage[...] = jnp.zeros_like(stage)
    copies[0].wait()
    copies[1].wait()
    patch = patch_ref[...]
    span = span_ref[...]
    owner = ((patch.astype(F32) + 0.5) * (1.0 / PATCH_DEV)).astype(I32)
    local = patch - owner * PATCH_DEV
    code_ref[...] = ((span & 1) * TABLE + (span >> 1) * PITCH + local).astype(F32)
    upper = (iota((128, 128), 0) < iota((128, 128), 1)).astype(F32)
    upper = jnp.concatenate([upper, jnp.ones((128, 128), F32)], 1).astype(BF16)
    lower = (iota((64, 64), 0) > iota((64, 64), 1)).astype(F32).astype(BF16)
    lane = iota((64, 128), 1)
    begin = jnp.zeros((64, 128), F32)
    counts = jnp.zeros((64, 128), F32)
    place = jnp.zeros((128, 128), F32)
    for o in range(OWNERS):
        mine = owner == o
        both = jnp.dot(mine.astype(F32).astype(BF16), upper, preferred_element_type=F32)
        earlier, total = both[:, :128], both[:, 128:]
        count = total[:64] + total[64:]
        place = jnp.where(
            mine, jnp.concatenate([earlier[:64] + begin, earlier[64:] + (total[:64] + begin)], 0), place)
        counts = jnp.where(lane == o, count, counts)
        begin = begin + count
    narrow = counts.astype(BF16)
    base = jnp.dot(lower, narrow, preferred_element_type=F32).astype(I32)
    first = jnp.dot(narrow, upper[:, :128], preferred_element_type=F32).astype(I32)
    offset = base & 127
    columns = (offset - first, offset, base >> 7, offset + counts.astype(I32), first)
    table = columns[0]
    for k, column in enumerate(columns[1:], 1):
        table = jnp.where(lane >= k * OWNERS, pltpu.roll(column, k * OWNERS, axis=1), table)
    place_ref[...] = place
    table_v[...] = table
    table_ref[...] = table
    copy = pltpu.make_async_copy(table_v, table_s, sem.at[4])
    copy.start()
    copies[2].wait()
    copies[3].wait()
    values[3:5, :] = (start_ref[...].astype(F32) + 0.5) * (1.0 / LEVELS)
    values[5:8, :] = jnp.zeros((3, values.shape[1]), F32)
    row = iota((8, 128), 0)
    lane = iota((8, 128), 1)

    def order(j):
        halves = []
        for h in range(2):
            r = j + 64 * h
            at = r * 128 if isinstance(r, int) else pl.multiple_of(r * 128, 128)
            x = values[:, pl.ds(at, 128)]
            halves.append(jnp.where(row == 5, code_ref[pl.ds(r, 8, stride=0), :], x))
        x = split3(jnp.concatenate(halves, 1))
        y = lax.dot_general(x, block_permutation(place_ref, j), (((1,), (1,)), ((), ())),
                            preferred_element_type=F32)
        return y[0:8] + y[8:16] + y[16:24]

    for step in range(STEPS):
        ordered[step] = order(step)
    copy.wait()

    def append(i, current):
        current = list(current)
        ready = [ordered[i * STEPS + step] for step in range(STEPS)]
        coming = [jnp.minimum((i + 1) * STEPS, 64 - STEPS) + step for step in range(STEPS)]
        for step in range(STEPS):
            j = i * STEPS + step
            y0, y1 = ready[step][:, 0:128], ready[step][:, 128:256]
            following = order(coming[step])
            for o in range(OWNERS):
                move, offset = table_s[j, o], table_s[j, 16 + o]
                tile, end = table_s[j, 32 + o], table_s[j, 48 + o]
                r0 = pltpu.roll(y0, move & 127, axis=1)
                r1 = pltpu.roll(y1, move & 127, axis=1)
                second = jnp.where(lane >= move, r1, r0)
                merged = jnp.where(lane >= offset, jnp.where(lane >= move + 128, r1, r0), current[o])
                at = pl.multiple_of((o * (TILES + MARGIN) + tile) * 8, 8)
                stage[pl.ds(at, 8), :] = merged
                stage[pl.ds(at + 8, 8), :] = second
                stage[pl.ds(at + 16, 8), :] = r1
                current[o] = jnp.where(end < 128, merged, jnp.where(end < 256, second, r1))
            ordered[coming[step]] = following
        return tuple(current)

    lax.fori_loop(0, 64 // STEPS, append, tuple(jnp.zeros((8, 128), F32) for _ in range(OWNERS)))
    for o in range(OWNERS):
        out_ref[o] = stage[pl.ds(o * (TILES + MARGIN) * 8, TILES * 8), :]


def dispatch(patch, span, start, target):
    vmem = pl.BlockSpec(memory_space=pltpu.VMEM)
    return pl.pallas_call(
        dispatch_kernel,
        out_shape=[
            jax.ShapeDtypeStruct((OWNERS, TILES * 8, 128), F32),
            jax.ShapeDtypeStruct((128, 128), F32),
            jax.ShapeDtypeStruct((64, 128), I32),
        ],
        in_specs=[pl.BlockSpec(memory_space=pl.ANY)] * 4,
        out_specs=[vmem] * 3,
        scratch_shapes=[
            pltpu.VMEM((128, 128), I32),
            pltpu.VMEM((128, 128), I32),
            pltpu.VMEM((2, 16384), I32),
            pltpu.VMEM((128, 128), F32),
            pltpu.VMEM((8, 16384), F32),
            pltpu.VMEM((64, 8, 256), F32),
            pltpu.VMEM((OWNERS * (TILES + MARGIN) * 8, 128), F32),
            pltpu.VMEM((64, 128), I32),
            pltpu.SMEM((64, 128), I32),
            pltpu.SemaphoreType.DMA((5,)),
        ],
        compiler_params=pltpu.CompilerParams(vmem_limit_bytes=62 << 20),
        name="dispatch",
    )(patch.reshape(128, 128), span.reshape(128, 128), start, target)


def centre(c0, c1, c2, c3):
    outer, inner = c0 + c3, c1 + c2
    outer_diff, inner_diff = c3 - c0, c2 - c1
    return (0.125 * outer + 0.375 * inner, 0.75 * (outer_diff + inner_diff),
            1.5 * (outer - inner), outer_diff - 3.0 * inner_diff)


def value_slope(a, t):
    b2 = a[3] * t + a[2]
    b1 = b2 * t + a[1]
    return b1 * t + a[0], (a[3] * t + b2) * t + b1


def value_only(a, t):
    return ((a[3] * t + a[2]) * t + a[1]) * t + a[0]


def surface(load, u, v):
    u, v = u - 0.5, v - 0.5
    point, along_u, along_v = [], [], []
    for c in range(4):
        values, slopes = [], []
        for j in range(4):
            value, slope = value_slope([load(c * 16 + i * 4 + j) for i in range(4)], u)
            values.append(value)
            slopes.append(slope)
        h, hv = value_slope(values, v)
        point.append(h)
        along_u.append(value_only(slopes, v))
        along_v.append(hv)
    inverse = 1.0 / point[3]
    p = [point[c] * inverse for c in range(3)]
    su = [(along_u[c] - p[c] * along_u[3]) * inverse for c in range(3)]
    sv = [(along_v[c] - p[c] * along_v[3]) * inverse for c in range(3)]
    return p, su, sv


def dot3(a, b):
    return a[0] * b[0] + a[1] * b[1] + a[2] * b[2]


def project(load, goal, u, v):
    for _ in range(ITERS):
        p, su, sv = surface(load, u, v)
        miss = [p[c] - goal[c] for c in range(3)]
        gu, gv = dot3(su, miss), dot3(sv, miss)
        a, d, b = dot3(su, su) + DAMPING, dot3(sv, sv) + DAMPING, dot3(su, sv)
        inverse = 1.0 / (a * d - b * b)
        u, v = (jnp.clip(u - (d * gu - b * gv) * inverse, 0.0, 1.0),
                jnp.clip(v - (a * gv - b * gu) * inverse, 0.0, 1.0))
    return surface(load, u, v)


def project_kernel(out_ref, net_hbm, main_ref, last_ref,
                   net, recv, index_v, index_a, index_b, rows_a, rows_b, turned, control_a, control_b,
                   main, last, last_pair,
                   net_sem, index_sem, own, send, arrive, back, home):
    me = lax.axis_index("bulk")
    barrier = pltpu.get_barrier_semaphore()
    for k in range(1, OWNERS):
        peer = lax.rem(me + k, OWNERS)
        pl.semaphore_signal(barrier, inc=1, device_id={"bulk": peer}, device_id_type=MESH)
    def net_copy(k):
        return pltpu.make_async_copy(
            net_hbm.at[:, pl.ds(pl.multiple_of(k * 128, 128), 128)],
            net.at[pl.ds(pl.multiple_of(k * PITCH, 8), PATCH_DEV), :], net_sem.at[k])

    for k in range(8):
        net_copy(k).start()
    first = pltpu.make_async_copy(out_ref.at[me], recv.at[pl.ds(0, SLOT), :], own.at[0])
    first.start()
    last[...] = jnp.zeros_like(last)
    pl.semaphore_wait(barrier, OWNERS - 1)

    def outward(k):
        peer = lax.rem(me + k, OWNERS)
        return pltpu.make_async_remote_copy(
            src_ref=out_ref.at[peer],
            dst_ref=recv.at[pl.ds(pl.multiple_of(k * SLOT, 8), SLOT), :],
            send_sem=send.at[k], recv_sem=arrive.at[k],
            device_id={"bulk": peer}, device_id_type=MESH,
        )

    def homeward(k, owner):
        peer = lax.rem(me + OWNERS - k, OWNERS)
        return [
            pltpu.make_async_remote_copy(
                src_ref=s.at[pl.ds(pl.multiple_of(k * n, 8), n), :],
                dst_ref=t.at[pl.ds(pl.multiple_of(owner * n, 8), n), :],
                send_sem=back.at[i, k], recv_sem=home.at[i, k],
                device_id={"bulk": peer}, device_id_type=MESH,
            )
            for i, (s, t, n) in enumerate(((main, main_ref, SLOT), (last, last_ref, 24)))
        ]

    stay = [
        pltpu.make_async_copy(main.at[pl.ds(0, SLOT), :],
                              main_ref.at[pl.ds(pl.multiple_of(me * SLOT, 8), SLOT), :], own.at[1]),
        pltpu.make_async_copy(last.at[pl.ds(0, 24), :],
                              last_ref.at[pl.ds(pl.multiple_of(me * 24, 8), 24), :], own.at[2]),
    ]

    def start_outward(k, carry):
        outward(k).start()
        return carry

    lax.fori_loop(1, OWNERS, start_outward, 0)

    def swap_halves(k, carry):
        net_copy(k).wait()
        for t in range(PITCH // 8):
            at = pl.multiple_of(k * PITCH + t * 8, 8)
            net[pl.ds(pl.multiple_of(at + TABLE, 8), 8), :] = pltpu.roll(net[pl.ds(at, 8), :], 64, axis=1)
        return carry

    lax.fori_loop(0, 8, swap_halves, 0)
    row, lane = iota((8, 128), 0), iota((8, 128), 1)
    masks = [[(row == s) & (lane < 64), (row == s) & (lane >= 64)] for s in range(8)]

    def prepare(m):
        for i in range(PAIR_BATCHES):
            b = m * PAIR_BATCHES + i
            code = recv[pl.ds(b * 64 + 5, 8, stride=8), :].astype(I32)
            code = jnp.clip(code, 0, 2 * TABLE - 1)
            swapped = jnp.where(code >= TABLE, code - TABLE, code + TABLE)
            index_v[b] = jnp.where((row & 1) == 1, swapped, code)

    def index_copy(b, half):
        return pltpu.make_async_copy(index_v.at[b], (index_a, index_b)[half], index_sem.at[half])

    def gather(index, rows):
        for h in range(4):
            for t in range(16):
                x = None
                for s in range(8):
                    for q in range(2):
                        w = net[pl.ds(index[2 * h + q, t * 8 + s], 8, stride=0), :]
                        x = w if x is None else jnp.where(masks[s][q], w, x)
                rows[pl.ds(h * 128 + t * 8, 8), :] = x

    def to_powers(rows, control):
        for h in range(4):
            both = rows[pl.ds(h * 128, 128), :].T
            turned[pl.ds(2 * h * TURN, 64), :] = both[:64]
            turned[pl.ds((2 * h + 1) * TURN, 64), :] = both[64:]
        for c in range(4):
            along = [
                centre(*[turned[pl.ds(c * 16 + i * 4 + j, 8, stride=TURN), :] for i in range(4)])
                for j in range(4)
            ]
            for i in range(4):
                for j, x in enumerate(centre(*[along[j][i] for j in range(4)])):
                    control[c * 16 + i * 4 + j] = x

    first.wait()
    outward(1).wait_recv()
    prepare(0)
    for half, (index, rows) in enumerate(((index_a, rows_a), (index_b, rows_b))):
        index_copy(half, half).start()
        index_copy(half, half).wait()
        gather(index, rows)
        index_copy(half + 2, half).start()
    to_powers(rows_a, control_a)

    def batch(b, half):
        index, rows, other, control, following = (
            (index_a, rows_a, rows_b, control_a, control_b),
            (index_b, rows_b, rows_a, control_b, control_a),
        )[half]
        m = lax.div(b, PAIR_BATCHES)
        i = b - m * PAIR_BATCHES
        index_copy(0, half).wait()
        gather(index, rows)
        to_powers(other, following)

        def load(k):
            return control[k]

        def value(k):
            return recv[pl.ds(b * 64 + k, 8, stride=8), :]

        p, su, sv = project(load, [value(0), value(1), value(2)], value(3), value(4))
        for k, x in enumerate((p + su + sv)[:8]):
            main[pl.ds(b * 64 + k, 8, stride=8), :] = x
        last_pair[pl.ds(pl.multiple_of(i * 8, 8), 8), :] = sv[2]

        @pl.when((i == 1) & (m < OWNERS // 2 - 1))
        def _():
            outward(2 * m + 2).wait_recv()
            outward(2 * m + 3).wait_recv()
            prepare(m + 1)

        index_copy(jnp.minimum(b + 4, BATCHES - 1), half).start()

        @pl.when(i == PAIR_BATCHES - 1)
        def _():
            for h in range(2):
                at = pl.multiple_of((2 * m + h) * 24, 8)
                last[pl.ds(at, TILES), :] = last_pair[h * TILES:(h + 1) * TILES, :]

            @pl.when(m == 0)
            def _():
                for copy in stay:
                    copy.start()

            @pl.when(m > 0)
            def _():
                for copy in homeward(2 * m, me):
                    copy.start()

            for copy in homeward(2 * m + 1, me):
                copy.start()

    def two(q, carry):
        batch(2 * q, 0)
        batch(2 * q + 1, 1)
        return carry

    lax.fori_loop(0, BATCHES // 2, two, 0)
    for half in range(2):
        index_copy(0, half).wait()
    for copy in stay:
        copy.wait()

    def finish(k, carry):
        outward(k).wait_send()
        for copy in homeward(k, lax.rem(me + k, OWNERS)):
            copy.wait()
        return carry

    lax.fori_loop(1, OWNERS, finish, 0)


def place_nodes(outgoing, net):
    vmem = pl.BlockSpec(memory_space=pltpu.VMEM)
    dma = pltpu.SemaphoreType.DMA
    return pl.pallas_call(
        project_kernel,
        out_shape=[
            jax.ShapeDtypeStruct((GROUPS * 8 + 24, 128), F32),
            jax.ShapeDtypeStruct((OWNERS * 24, 128), F32),
        ],
        in_specs=[vmem, pl.BlockSpec(memory_space=pl.ANY)],
        out_specs=[vmem] * 2,
        scratch_shapes=[
            pltpu.VMEM((2 * TABLE, 128), F32),
            pltpu.VMEM((GROUPS * 8 + 64, 128), F32),
            pltpu.VMEM((BATCHES, 8, 128), I32),
            pltpu.SMEM((8, 128), I32),
            pltpu.SMEM((8, 128), I32),
            pltpu.VMEM((BATCH * 64, 128), F32),
            pltpu.VMEM((BATCH * 64, 128), F32),
            pltpu.VMEM((BATCH * TURN + 64, 128), F32),
            pltpu.VMEM((64, 8, 128), F32),
            pltpu.VMEM((64, 8, 128), F32),
            pltpu.VMEM((GROUPS * 8 + 64, 128), F32),
            pltpu.VMEM((OWNERS * 24, 128), F32),
            pltpu.VMEM((2 * TILES, 128), F32),
            dma((8,)), dma((2,)), dma((3,)),
            dma((OWNERS,)), dma((OWNERS,)), dma((2, OWNERS)), dma((2, OWNERS)),
        ],
        compiler_params=pltpu.CompilerParams(
            collective_id=1, has_side_effects=True, vmem_limit_bytes=48 << 20),
        name="project",
    )(outgoing, net)


def collect_kernel(main, last, place_ref, table_hbm, out_ref, ordered, table_s, sem):
    copy = pltpu.make_async_copy(table_hbm, table_s, sem)
    copy.start()
    copy.wait()
    lane = iota((8, 128), 1)

    def assemble(j):
        acc = [jnp.zeros((8, 128), F32) for _ in range(4)]
        for o in range(OWNERS):
            move, offset = table_s[j, o], table_s[j, 16 + o]
            tile, first = table_s[j, 32 + o], table_s[j, 64 + o]
            at = pl.multiple_of((o * TILES + tile) * 8, 8)
            at_last = o * 24 + tile
            keep = lane >= offset
            in_low, in_high = lane >= first, lane >= first - 128
            from_low = lane >= 128 - move
            from_high = (lane >= -move) & (lane < 128 - move)
            windows = (
                [main[pl.ds(at + 8 * k, 8), :] for k in range(3)],
                [last[pl.ds(at_last + k, 8, stride=0), :] for k in range(3)],
            )
            for k, (w0, w1, w2) in enumerate(windows):
                r0 = pltpu.roll(jnp.where(keep, w0, w2), (-move) & 127, axis=1)
                r1 = pltpu.roll(w1, (-move) & 127, axis=1)
                acc[2 * k] = jnp.where(in_low, jnp.where(from_low, r1, r0), acc[2 * k])
                acc[2 * k + 1] = jnp.where(in_high, jnp.where(from_high, r1, r0), acc[2 * k + 1])
        return acc

    def keep_block(j, acc):
        for k in range(2):
            ordered[j, 8 * k:8 * k + 8, 0:128] = acc[2 * k]
            ordered[j, 8 * k:8 * k + 8, 128:256] = acc[2 * k + 1]

    for step in range(STEPS):
        keep_block(step, assemble(step))

    def spread(i, carry):
        ready = [ordered[i * STEPS + step] for step in range(STEPS)]
        for step in range(STEPS):
            j = i * STEPS + step
            y = jnp.dot(split3(ready[step]), block_permutation(place_ref, j), preferred_element_type=F32)
            y = y[0:16] + y[16:32] + y[32:48]
            for h in range(2):
                at = pl.multiple_of((j + 64 * h) * 128, 128)
                out_ref[:, pl.ds(at, 128)] = y[0:9, h * 128:(h + 1) * 128]
            coming = jnp.minimum((i + 1) * STEPS, 64 - STEPS) + step
            keep_block(coming, assemble(coming))
        return carry

    lax.fori_loop(0, 64 // STEPS, spread, 0)


def collect(main, last, place, table):
    vmem = pl.BlockSpec(memory_space=pltpu.VMEM)
    hbm = pl.BlockSpec(memory_space=pl.ANY)
    return pl.pallas_call(
        collect_kernel,
        out_shape=jax.ShapeDtypeStruct((9, 16384), F32),
        in_specs=[vmem, vmem, vmem, hbm],
        out_specs=vmem,
        scratch_shapes=[pltpu.VMEM((64, 16, 256), F32), pltpu.SMEM((64, 128), I32), pltpu.SemaphoreType.DMA],
        compiler_params=pltpu.CompilerParams(vmem_limit_bytes=32 << 20),
        name="collect",
    )(main, last, place, table)


def body(node_patch, node_span, start_grid, target, net):
    outgoing, place, table = dispatch(node_patch, node_span, start_grid, target)
    main, last = place_nodes(outgoing, net)
    return collect(main, last, place, table)


def solution(mesh):
    return jax.shard_map(
        body,
        mesh=mesh,
        in_specs=(
            P(("dom", "bulk")),
            P(("dom", "bulk")),
            P(None, ("dom", "bulk")),
            P(None, ("dom", "bulk")),
            P("bulk", None),
        ),
        out_specs=P(None, ("dom", "bulk")),
        check_vma=False,
    )
```

```python
import jax
import jax.numpy as jnp
from jax import lax
from jax.experimental import pallas as pl
from jax.experimental.pallas import tpu as pltpu
from jax.sharding import PartitionSpec as P

F32 = jnp.float32
BF16 = jnp.bfloat16
I32 = jnp.int32
MESH = pl.DeviceIdType.MESH

SPANS = 16
LEVELS = 16
ITERS = 4
DAMPING = 0.1
OWNERS = 16
PATCH_DEV = 2500
PITCH = 2504
TABLE = 8 * PITCH
TILES = 20
GROUPS = OWNERS * TILES
MARGIN = 3
OWN = OWNERS - 1
FILL = 5
STEPS = 4
BATCH = 8
TURN = 72
SLOT = TILES * 8
PAIR_BATCHES = 2 * TILES // BATCH
BATCHES = GROUPS // BATCH


def iota(shape, dim):
    return lax.broadcasted_iota(I32, shape, dim)


def split3(x):
    high = x.astype(BF16)
    rest = x - high.astype(F32)
    mid = rest.astype(BF16)
    low = (rest - mid.astype(F32)).astype(BF16)
    return jnp.concatenate([high, mid, low], 0)


def block_permutation(place_ref, j):
    place = jnp.concatenate([place_ref[pl.ds(j, 1), :], place_ref[pl.ds(j + 64, 1), :]], 1)
    return jnp.where(iota((256, 256), 0).astype(F32) == place, 1.0, 0.0).astype(BF16)


def dispatch_kernel(patch_hbm, span_hbm, start_hbm, target_hbm, out_ref, place_ref, table_ref,
                    patch_ref, span_ref, start_ref, code_ref, values, ordered, stage, table_v, table_s, sem):
    copies = [
        pltpu.make_async_copy(patch_hbm, patch_ref, sem.at[0]),
        pltpu.make_async_copy(span_hbm, span_ref, sem.at[1]),
        pltpu.make_async_copy(start_hbm, start_ref, sem.at[2]),
        pltpu.make_async_copy(target_hbm, values.at[pl.ds(0, 3), :], sem.at[3]),
    ]
    for copy in copies:
        copy.start()
    stage[...] = jnp.zeros_like(stage)
    copies[0].wait()
    copies[1].wait()
    patch = patch_ref[...]
    span = span_ref[...]
    owner = ((patch.astype(F32) + 0.5) * (1.0 / PATCH_DEV)).astype(I32)
    local = patch - owner * PATCH_DEV
    code_ref[...] = ((span & 1) * TABLE + (span >> 1) * PITCH + local).astype(F32)
    upper = (iota((128, 128), 0) < iota((128, 128), 1)).astype(F32)
    upper = jnp.concatenate([upper, jnp.ones((128, 128), F32)], 1).astype(BF16)
    lower = (iota((64, 64), 0) > iota((64, 64), 1)).astype(F32).astype(BF16)
    lane = iota((64, 128), 1)
    begin = jnp.zeros((64, 128), F32)
    counts = jnp.zeros((64, 128), F32)
    place = jnp.zeros((128, 128), F32)
    for o in range(OWNERS):
        mine = owner == o
        both = jnp.dot(mine.astype(F32).astype(BF16), upper, preferred_element_type=F32)
        earlier, total = both[:, :128], both[:, 128:]
        count = total[:64] + total[64:]
        place = jnp.where(
            mine, jnp.concatenate([earlier[:64] + begin, earlier[64:] + (total[:64] + begin)], 0), place)
        counts = jnp.where(lane == o, count, counts)
        begin = begin + count
    narrow = counts.astype(BF16)
    base = jnp.dot(lower, narrow, preferred_element_type=F32).astype(I32)
    first = jnp.dot(narrow, upper[:, :128], preferred_element_type=F32).astype(I32)
    offset = base & 127
    columns = (offset - first, offset, base >> 7, offset + counts.astype(I32), first)
    table = columns[0]
    for k, column in enumerate(columns[1:], 1):
        table = jnp.where(lane >= k * OWNERS, pltpu.roll(column, k * OWNERS, axis=1), table)
    place_ref[...] = place
    table_v[...] = table
    table_ref[...] = table
    copy = pltpu.make_async_copy(table_v, table_s, sem.at[4])
    copy.start()
    copies[2].wait()
    copies[3].wait()
    values[3:5, :] = (start_ref[...].astype(F32) + 0.5) * (1.0 / LEVELS)
    values[5:8, :] = jnp.zeros((3, values.shape[1]), F32)
    row = iota((8, 128), 0)
    lane = iota((8, 128), 1)

    def order(j):
        halves = []
        for h in range(2):
            r = j + 64 * h
            at = r * 128 if isinstance(r, int) else pl.multiple_of(r * 128, 128)
            x = values[:, pl.ds(at, 128)]
            halves.append(jnp.where(row == 5, code_ref[pl.ds(r, 8, stride=0), :], x))
        x = split3(jnp.concatenate(halves, 1))
        y = lax.dot_general(x, block_permutation(place_ref, j), (((1,), (1,)), ((), ())),
                            preferred_element_type=F32)
        return y[0:8] + y[8:16] + y[16:24]

    for step in range(STEPS):
        ordered[step] = order(step)
    copy.wait()

    def append(i, current):
        current = list(current)
        ready = [ordered[i * STEPS + step] for step in range(STEPS)]
        coming = [jnp.minimum((i + 1) * STEPS, 64 - STEPS) + step for step in range(STEPS)]
        for step in range(STEPS):
            j = i * STEPS + step
            y0, y1 = ready[step][:, 0:128], ready[step][:, 128:256]
            following = order(coming[step])
            for o in range(OWNERS):
                move, offset = table_s[j, o], table_s[j, 16 + o]
                tile, end = table_s[j, 32 + o], table_s[j, 48 + o]
                r0 = pltpu.roll(y0, move & 127, axis=1)
                r1 = pltpu.roll(y1, move & 127, axis=1)
                second = jnp.where(lane >= move, r1, r0)
                merged = jnp.where(lane >= offset, jnp.where(lane >= move + 128, r1, r0), current[o])
                at = pl.multiple_of((o * (TILES + MARGIN) + tile) * 8, 8)
                stage[pl.ds(at, 8), :] = merged
                stage[pl.ds(at + 8, 8), :] = second
                stage[pl.ds(at + 16, 8), :] = r1
                current[o] = jnp.where(end < 128, merged, jnp.where(end < 256, second, r1))
            ordered[coming[step]] = following
        return tuple(current)

    lax.fori_loop(0, 64 // STEPS, append, tuple(jnp.zeros((8, 128), F32) for _ in range(OWNERS)))
    for o in range(OWNERS):
        out_ref[o] = stage[pl.ds(o * (TILES + MARGIN) * 8, TILES * 8), :]


def dispatch(patch, span, start, target):
    vmem = pl.BlockSpec(memory_space=pltpu.VMEM)
    return pl.pallas_call(
        dispatch_kernel,
        out_shape=[
            jax.ShapeDtypeStruct((OWNERS, TILES * 8, 128), F32),
            jax.ShapeDtypeStruct((128, 128), F32),
            jax.ShapeDtypeStruct((64, 128), I32),
        ],
        in_specs=[pl.BlockSpec(memory_space=pl.ANY)] * 4,
        out_specs=[vmem] * 3,
        scratch_shapes=[
            pltpu.VMEM((128, 128), I32),
            pltpu.VMEM((128, 128), I32),
            pltpu.VMEM((2, 16384), I32),
            pltpu.VMEM((128, 128), F32),
            pltpu.VMEM((8, 16384), F32),
            pltpu.VMEM((64, 8, 256), F32),
            pltpu.VMEM((OWNERS * (TILES + MARGIN) * 8, 128), F32),
            pltpu.VMEM((64, 128), I32),
            pltpu.SMEM((64, 128), I32),
            pltpu.SemaphoreType.DMA((5,)),
        ],
        compiler_params=pltpu.CompilerParams(vmem_limit_bytes=62 << 20),
        name="dispatch",
    )(patch.reshape(128, 128), span.reshape(128, 128), start, target)


def centre(c0, c1, c2, c3):
    outer, inner = c0 + c3, c1 + c2
    outer_diff, inner_diff = c3 - c0, c2 - c1
    return (0.125 * outer + 0.375 * inner, 0.75 * (outer_diff + inner_diff),
            1.5 * (outer - inner), outer_diff - 3.0 * inner_diff)


def value_slope(a, t):
    b2 = a[3] * t + a[2]
    b1 = b2 * t + a[1]
    return b1 * t + a[0], (a[3] * t + b2) * t + b1


def value_only(a, t):
    return ((a[3] * t + a[2]) * t + a[1]) * t + a[0]


def surface(load, u, v):
    u, v = u - 0.5, v - 0.5
    point, along_u, along_v = [], [], []
    for c in range(4):
        values, slopes = [], []
        for j in range(4):
            value, slope = value_slope([load(c * 16 + i * 4 + j) for i in range(4)], u)
            values.append(value)
            slopes.append(slope)
        h, hv = value_slope(values, v)
        point.append(h)
        along_u.append(value_only(slopes, v))
        along_v.append(hv)
    inverse = 1.0 / point[3]
    p = [point[c] * inverse for c in range(3)]
    su = [(along_u[c] - p[c] * along_u[3]) * inverse for c in range(3)]
    sv = [(along_v[c] - p[c] * along_v[3]) * inverse for c in range(3)]
    return p, su, sv


def dot3(a, b):
    return a[0] * b[0] + a[1] * b[1] + a[2] * b[2]


def project(load, goal, u, v, between):
    for _ in range(ITERS):
        p, su, sv = surface(load, u, v)
        miss = [p[c] - goal[c] for c in range(3)]
        gu, gv = dot3(su, miss), dot3(sv, miss)
        a, d, b = dot3(su, su) + DAMPING, dot3(sv, sv) + DAMPING, dot3(su, sv)
        inverse = 1.0 / (a * d - b * b)
        u, v = (jnp.clip(u - (d * gu - b * gv) * inverse, 0.0, 1.0),
                jnp.clip(v - (a * gv - b * gu) * inverse, 0.0, 1.0))
        between()
    return surface(load, u, v)


def project_kernel(out_ref, net_hbm, main_ref, last_ref,
                   net, recv, index_v, index_a, index_b, rows_a, rows_b, turned, control_a, control_b,
                   main, last, last_pair,
                   net_sem, index_sem, own, send, arrive, back, home):
    me = lax.axis_index("bulk")
    barrier = pltpu.get_barrier_semaphore()
    for k in range(1, OWNERS):
        peer = lax.rem(me + k, OWNERS)
        pl.semaphore_signal(barrier, inc=1, device_id={"bulk": peer}, device_id_type=MESH)
    def net_copy(k):
        return pltpu.make_async_copy(
            net_hbm.at[:, pl.ds(pl.multiple_of(k * 128, 128), 128)],
            net.at[pl.ds(pl.multiple_of(k * PITCH, 8), PATCH_DEV), :], net_sem.at[k])

    for k in range(8):
        net_copy(k).start()
    first = pltpu.make_async_copy(out_ref.at[me], recv.at[pl.ds(OWN * SLOT, SLOT), :], own.at[0])
    first.start()
    last[...] = jnp.zeros_like(last)
    pl.semaphore_wait(barrier, OWNERS - 1)

    def outward(k):
        peer = lax.rem(me + k, OWNERS)
        return pltpu.make_async_remote_copy(
            src_ref=out_ref.at[peer],
            dst_ref=recv.at[pl.ds(pl.multiple_of((k - 1) * SLOT, 8), SLOT), :],
            send_sem=send.at[k], recv_sem=arrive.at[k],
            device_id={"bulk": peer}, device_id_type=MESH,
        )

    def homeward(k, owner):
        peer = lax.rem(me + OWNERS - k, OWNERS)
        return [
            pltpu.make_async_remote_copy(
                src_ref=s.at[pl.ds(pl.multiple_of((k - 1) * n, 8), n), :],
                dst_ref=t.at[pl.ds(pl.multiple_of(owner * n, 8), n), :],
                send_sem=back.at[i, k], recv_sem=home.at[i, k],
                device_id={"bulk": peer}, device_id_type=MESH,
            )
            for i, (s, t, n) in enumerate(((main, main_ref, SLOT), (last, last_ref, 24)))
        ]

    stay = [
        pltpu.make_async_copy(main.at[pl.ds(OWN * SLOT, SLOT), :],
                              main_ref.at[pl.ds(pl.multiple_of(me * SLOT, 8), SLOT), :], own.at[1]),
        pltpu.make_async_copy(last.at[pl.ds(OWN * 24, 24), :],
                              last_ref.at[pl.ds(pl.multiple_of(me * 24, 8), 24), :], own.at[2]),
    ]

    def start_outward(k, carry):
        outward(k).start()
        return carry

    lax.fori_loop(1, OWNERS, start_outward, 0)

    def swap_halves(k, carry):
        net_copy(k).wait()
        for t in range(PITCH // 8):
            at = pl.multiple_of(k * PITCH + t * 8, 8)
            net[pl.ds(pl.multiple_of(at + TABLE, 8), 8), :] = pltpu.roll(net[pl.ds(at, 8), :], 64, axis=1)
        return carry

    lax.fori_loop(0, 8, swap_halves, 0)
    row, lane = iota((8, 128), 0), iota((8, 128), 1)
    masks = [[(row == s) & (lane < 64), (row == s) & (lane >= 64)] for s in range(8)]

    def prepare(m):
        for i in range(PAIR_BATCHES):
            b = m * PAIR_BATCHES + i
            code = recv[pl.ds(b * 64 + 5, 8, stride=8), :].astype(I32)
            code = jnp.clip(code, 0, 2 * TABLE - 1)
            swapped = jnp.where(code >= TABLE, code - TABLE, code + TABLE)
            index_v[b] = jnp.where((row & 1) == 1, swapped, code)

    def index_copy(b, half):
        return pltpu.make_async_copy(index_v.at[b], (index_a, index_b)[half], index_sem.at[half])

    def gather(index, rows, begin, end):
        for unit in range(begin, end):
            h, t = divmod(unit, 16)
            x = None
            for s in range(8):
                for q in range(2):
                    w = net[pl.ds(index[2 * h + q, t * 8 + s], 8, stride=0), :]
                    x = w if x is None else jnp.where(masks[s][q], w, x)
            rows[pl.ds(h * 128 + t * 8, 8), :] = x

    def to_powers(rows, control, between):
        for h in range(4):
            both = rows[pl.ds(h * 128, 128), :].T
            turned[pl.ds(2 * h * TURN, 64), :] = both[:64]
            turned[pl.ds((2 * h + 1) * TURN, 64), :] = both[64:]
            between()
        for c in range(4):
            along = [
                centre(*[turned[pl.ds(c * 16 + i * 4 + j, 8, stride=TURN), :] for i in range(4)])
                for j in range(4)
            ]
            for i in range(4):
                for j, x in enumerate(centre(*[along[j][i] for j in range(4)])):
                    control[c * 16 + i * 4 + j] = x
            between()

    first.wait()
    outward(1).wait_recv()
    outward(2).wait_recv()
    prepare(0)
    for half, (index, rows) in enumerate(((index_a, rows_a), (index_b, rows_b))):
        index_copy(half, half).start()
        index_copy(half, half).wait()
        gather(index, rows, 0, 64)
        index_copy(half + 2, half).start()
    to_powers(rows_a, control_a, lambda: None)

    def batch(b, half):
        index, rows, other, control, following = (
            (index_a, rows_a, rows_b, control_a, control_b),
            (index_b, rows_b, rows_a, control_b, control_a),
        )[half]
        m = lax.div(b, PAIR_BATCHES)
        i = b - m * PAIR_BATCHES
        index_copy(0, half).wait()
        cuts = iter(range(0, 64, FILL))

        def between():
            at = next(cuts, 64)
            gather(index, rows, at, min(at + FILL, 64))

        to_powers(other, following, between)

        def load(k):
            return control[k]

        def value(k):
            return recv[pl.ds(b * 64 + k, 8, stride=8), :]

        p, su, sv = project(load, [value(0), value(1), value(2)], value(3), value(4), between)
        for k, x in enumerate((p + su + sv)[:8]):
            main[pl.ds(b * 64 + k, 8, stride=8), :] = x
        last_pair[pl.ds(pl.multiple_of(i * 8, 8), 8), :] = sv[2]
        between()

        @pl.when((i == 1) & (m < OWNERS // 2 - 1))
        def _():
            outward(2 * m + 3).wait_recv()

            @pl.when(m < OWNERS // 2 - 2)
            def _():
                outward(2 * m + 4).wait_recv()

            prepare(m + 1)

        index_copy(jnp.minimum(b + 4, BATCHES - 1), half).start()

        def keep_last(h):
            at = pl.multiple_of((2 * m + h) * 24, 8)
            last[pl.ds(at, TILES), :] = last_pair[h * TILES:(h + 1) * TILES, :]

        @pl.when(i == 2)
        def _():
            keep_last(0)
            for copy in homeward(2 * m + 1, me):
                copy.start()

        @pl.when(i == PAIR_BATCHES - 1)
        def _():
            keep_last(1)

            @pl.when(m < OWNERS // 2 - 1)
            def _():
                for copy in homeward(2 * m + 2, me):
                    copy.start()

            @pl.when(m == OWNERS // 2 - 1)
            def _():
                for copy in stay:
                    copy.start()

    def two(q, carry):
        batch(2 * q, 0)
        batch(2 * q + 1, 1)
        return carry

    lax.fori_loop(0, BATCHES // 2, two, 0)
    for half in range(2):
        index_copy(0, half).wait()
    for copy in stay:
        copy.wait()

    def finish(k, carry):
        outward(k).wait_send()
        for copy in homeward(k, lax.rem(me + k, OWNERS)):
            copy.wait()
        return carry

    lax.fori_loop(1, OWNERS, finish, 0)


def place_nodes(outgoing, net):
    vmem = pl.BlockSpec(memory_space=pltpu.VMEM)
    dma = pltpu.SemaphoreType.DMA
    return pl.pallas_call(
        project_kernel,
        out_shape=[
            jax.ShapeDtypeStruct((GROUPS * 8 + 24, 128), F32),
            jax.ShapeDtypeStruct((OWNERS * 24, 128), F32),
        ],
        in_specs=[vmem, pl.BlockSpec(memory_space=pl.ANY)],
        out_specs=[vmem] * 2,
        scratch_shapes=[
            pltpu.VMEM((2 * TABLE, 128), F32),
            pltpu.VMEM((GROUPS * 8 + 64, 128), F32),
            pltpu.VMEM((BATCHES, 8, 128), I32),
            pltpu.SMEM((8, 128), I32),
            pltpu.SMEM((8, 128), I32),
            pltpu.VMEM((BATCH * 64, 128), F32),
            pltpu.VMEM((BATCH * 64, 128), F32),
            pltpu.VMEM((BATCH * TURN + 64, 128), F32),
            pltpu.VMEM((64, 8, 128), F32),
            pltpu.VMEM((64, 8, 128), F32),
            pltpu.VMEM((GROUPS * 8 + 64, 128), F32),
            pltpu.VMEM((OWNERS * 24, 128), F32),
            pltpu.VMEM((2 * TILES, 128), F32),
            dma((8,)), dma((2,)), dma((3,)),
            dma((OWNERS,)), dma((OWNERS,)), dma((2, OWNERS)), dma((2, OWNERS)),
        ],
        compiler_params=pltpu.CompilerParams(
            collective_id=1, has_side_effects=True, vmem_limit_bytes=48 << 20),
        name="project",
    )(outgoing, net)


def collect_kernel(main, last, place_ref, table_hbm, out_ref, ordered, table_s, sem):
    copy = pltpu.make_async_copy(table_hbm, table_s, sem)
    copy.start()
    copy.wait()
    lane = iota((8, 128), 1)

    def assemble(j):
        acc = [jnp.zeros((8, 128), F32) for _ in range(4)]
        for o in range(OWNERS):
            move, offset = table_s[j, o], table_s[j, 16 + o]
            tile, first = table_s[j, 32 + o], table_s[j, 64 + o]
            at = pl.multiple_of((o * TILES + tile) * 8, 8)
            at_last = o * 24 + tile
            keep = lane >= offset
            in_low, in_high = lane >= first, lane >= first - 128
            from_low = lane >= 128 - move
            from_high = (lane >= -move) & (lane < 128 - move)
            windows = (
                [main[pl.ds(at + 8 * k, 8), :] for k in range(3)],
                [last[pl.ds(at_last + k, 8, stride=0), :] for k in range(3)],
            )
            for k, (w0, w1, w2) in enumerate(windows):
                r0 = pltpu.roll(jnp.where(keep, w0, w2), (-move) & 127, axis=1)
                r1 = pltpu.roll(w1, (-move) & 127, axis=1)
                acc[2 * k] = jnp.where(in_low, jnp.where(from_low, r1, r0), acc[2 * k])
                acc[2 * k + 1] = jnp.where(in_high, jnp.where(from_high, r1, r0), acc[2 * k + 1])
        return acc

    def keep_block(j, acc):
        for k in range(2):
            ordered[j, 8 * k:8 * k + 8, 0:128] = acc[2 * k]
            ordered[j, 8 * k:8 * k + 8, 128:256] = acc[2 * k + 1]

    for step in range(STEPS):
        keep_block(step, assemble(step))

    def spread(i, carry):
        ready = [ordered[i * STEPS + step] for step in range(STEPS)]
        for step in range(STEPS):
            j = i * STEPS + step
            y = jnp.dot(split3(ready[step]), block_permutation(place_ref, j), preferred_element_type=F32)
            y = y[0:16] + y[16:32] + y[32:48]
            for h in range(2):
                at = pl.multiple_of((j + 64 * h) * 128, 128)
                out_ref[:, pl.ds(at, 128)] = y[0:9, h * 128:(h + 1) * 128]
            coming = jnp.minimum((i + 1) * STEPS, 64 - STEPS) + step
            keep_block(coming, assemble(coming))
        return carry

    lax.fori_loop(0, 64 // STEPS, spread, 0)


def collect(main, last, place, table):
    vmem = pl.BlockSpec(memory_space=pltpu.VMEM)
    hbm = pl.BlockSpec(memory_space=pl.ANY)
    return pl.pallas_call(
        collect_kernel,
        out_shape=jax.ShapeDtypeStruct((9, 16384), F32),
        in_specs=[vmem, vmem, vmem, hbm],
        out_specs=vmem,
        scratch_shapes=[pltpu.VMEM((64, 16, 256), F32), pltpu.SMEM((64, 128), I32), pltpu.SemaphoreType.DMA],
        compiler_params=pltpu.CompilerParams(vmem_limit_bytes=32 << 20),
        name="collect",
    )(main, last, place, table)


def body(node_patch, node_span, start_grid, target, net):
    outgoing, place, table = dispatch(node_patch, node_span, start_grid, target)
    main, last = place_nodes(outgoing, net)
    return collect(main, last, place, table)


def solution(mesh):
    return jax.shard_map(
        body,
        mesh=mesh,
        in_specs=(
            P(("dom", "bulk")),
            P(("dom", "bulk")),
            P(None, ("dom", "bulk")),
            P(None, ("dom", "bulk")),
            P("bulk", None),
        ),
        out_specs=P(None, ("dom", "bulk")),
        check_vma=False,
    )
```

```python
import jax
import jax.numpy as jnp
from jax import lax
from jax.experimental import pallas as pl
from jax.experimental.pallas import tpu as pltpu
from jax.sharding import PartitionSpec as P

F32 = jnp.float32
BF16 = jnp.bfloat16
I32 = jnp.int32
MESH = pl.DeviceIdType.MESH

SPANS = 16
LEVELS = 16
ITERS = 4
DAMPING = 0.1
OWNERS = 16
PATCH_DEV = 2500
PITCH = 2504
TABLE = 8 * PITCH
TILES = 20
GROUPS = OWNERS * TILES
MARGIN = 3
OWN = OWNERS - 1
FILL = 5
STEPS = 4
BATCH = 8
TURN = 72
SLOT = TILES * 8
PAIR_BATCHES = 2 * TILES // BATCH
BATCHES = GROUPS // BATCH


def iota(shape, dim):
    return lax.broadcasted_iota(I32, shape, dim)


def split3(x):
    high = x.astype(BF16)
    rest = x - high.astype(F32)
    mid = rest.astype(BF16)
    low = (rest - mid.astype(F32)).astype(BF16)
    return jnp.concatenate([high, mid, low], 0)


def block_permutation(place_ref, j):
    place = jnp.concatenate([place_ref[pl.ds(j, 1), :], place_ref[pl.ds(j + 64, 1), :]], 1)
    return jnp.where(iota((256, 256), 0).astype(F32) == place, 1.0, 0.0).astype(BF16)


def dispatch_kernel(patch_hbm, span_hbm, start_hbm, target_hbm, out_ref, place_ref, table_ref,
                    patch_ref, span_ref, start_ref, code_ref, values, ordered, stage, table_v, table_s, sem):
    copies = [
        pltpu.make_async_copy(patch_hbm, patch_ref, sem.at[0]),
        pltpu.make_async_copy(span_hbm, span_ref, sem.at[1]),
        pltpu.make_async_copy(start_hbm, start_ref, sem.at[2]),
        pltpu.make_async_copy(target_hbm, values.at[pl.ds(0, 3), :], sem.at[3]),
    ]
    for copy in copies:
        copy.start()
    stage[...] = jnp.zeros_like(stage)
    copies[0].wait()
    copies[1].wait()
    patch = patch_ref[...]
    span = span_ref[...]
    owner = ((patch.astype(F32) + 0.5) * (1.0 / PATCH_DEV)).astype(I32)
    local = patch - owner * PATCH_DEV
    code_ref[...] = ((span & 1) * TABLE + (span >> 1) * PITCH + local).astype(F32)
    upper = (iota((128, 128), 0) < iota((128, 128), 1)).astype(F32)
    upper = jnp.concatenate([upper, jnp.ones((128, 128), F32)], 1).astype(BF16)
    lower = (iota((64, 64), 0) > iota((64, 64), 1)).astype(F32).astype(BF16)
    lane = iota((64, 128), 1)
    begin = jnp.zeros((64, 128), F32)
    counts = jnp.zeros((64, 128), F32)
    place = jnp.zeros((128, 128), F32)
    for o in range(OWNERS):
        mine = owner == o
        both = jnp.dot(mine.astype(F32).astype(BF16), upper, preferred_element_type=F32)
        earlier, total = both[:, :128], both[:, 128:]
        count = total[:64] + total[64:]
        place = jnp.where(
            mine, jnp.concatenate([earlier[:64] + begin, earlier[64:] + (total[:64] + begin)], 0), place)
        counts = jnp.where(lane == o, count, counts)
        begin = begin + count
    narrow = counts.astype(BF16)
    base = jnp.dot(lower, narrow, preferred_element_type=F32).astype(I32)
    first = jnp.dot(narrow, upper[:, :128], preferred_element_type=F32).astype(I32)
    offset = base & 127
    columns = (offset - first, offset, base >> 7, offset + counts.astype(I32), first)
    table = columns[0]
    for k, column in enumerate(columns[1:], 1):
        table = jnp.where(lane >= k * OWNERS, pltpu.roll(column, k * OWNERS, axis=1), table)
    place_ref[...] = place
    table_v[...] = table
    table_ref[...] = table
    copy = pltpu.make_async_copy(table_v, table_s, sem.at[4])
    copy.start()
    copies[2].wait()
    copies[3].wait()
    values[3:5, :] = (start_ref[...].astype(F32) + 0.5) * (1.0 / LEVELS)
    values[5:8, :] = jnp.zeros((3, values.shape[1]), F32)
    row = iota((8, 128), 0)
    lane = iota((8, 128), 1)

    def order(j):
        halves = []
        for h in range(2):
            r = j + 64 * h
            at = r * 128 if isinstance(r, int) else pl.multiple_of(r * 128, 128)
            x = values[:, pl.ds(at, 128)]
            halves.append(jnp.where(row == 5, code_ref[pl.ds(r, 8, stride=0), :], x))
        x = split3(jnp.concatenate(halves, 1))
        y = lax.dot_general(x, block_permutation(place_ref, j), (((1,), (1,)), ((), ())),
                            preferred_element_type=F32)
        return y[0:8] + y[8:16] + y[16:24]

    for step in range(STEPS):
        ordered[step] = order(step)
    copy.wait()

    def append(i, current):
        current = list(current)
        ready = [ordered[i * STEPS + step] for step in range(STEPS)]
        coming = [jnp.minimum((i + 1) * STEPS, 64 - STEPS) + step for step in range(STEPS)]
        for step in range(STEPS):
            j = i * STEPS + step
            y0, y1 = ready[step][:, 0:128], ready[step][:, 128:256]
            following = order(coming[step])
            for o in range(OWNERS):
                move, offset = table_s[j, o], table_s[j, 16 + o]
                tile, end = table_s[j, 32 + o], table_s[j, 48 + o]
                r0 = pltpu.roll(y0, move & 127, axis=1)
                r1 = pltpu.roll(y1, move & 127, axis=1)
                second = jnp.where(lane >= move, r1, r0)
                merged = jnp.where(lane >= offset, jnp.where(lane >= move + 128, r1, r0), current[o])
                at = pl.multiple_of((o * (TILES + MARGIN) + tile) * 8, 8)
                stage[pl.ds(at, 8), :] = merged
                stage[pl.ds(at + 8, 8), :] = second
                stage[pl.ds(at + 16, 8), :] = r1
                current[o] = jnp.where(end < 128, merged, jnp.where(end < 256, second, r1))
            ordered[coming[step]] = following
        return tuple(current)

    lax.fori_loop(0, 64 // STEPS, append, tuple(jnp.zeros((8, 128), F32) for _ in range(OWNERS)))
    for o in range(OWNERS):
        out_ref[o] = stage[pl.ds(o * (TILES + MARGIN) * 8, TILES * 8), :]


def dispatch(patch, span, start, target):
    vmem = pl.BlockSpec(memory_space=pltpu.VMEM)
    return pl.pallas_call(
        dispatch_kernel,
        out_shape=[
            jax.ShapeDtypeStruct((OWNERS, TILES * 8, 128), F32),
            jax.ShapeDtypeStruct((128, 128), F32),
            jax.ShapeDtypeStruct((64, 128), I32),
        ],
        in_specs=[pl.BlockSpec(memory_space=pl.ANY)] * 4,
        out_specs=[vmem] * 3,
        scratch_shapes=[
            pltpu.VMEM((128, 128), I32),
            pltpu.VMEM((128, 128), I32),
            pltpu.VMEM((2, 16384), I32),
            pltpu.VMEM((128, 128), F32),
            pltpu.VMEM((8, 16384), F32),
            pltpu.VMEM((64, 8, 256), F32),
            pltpu.VMEM((OWNERS * (TILES + MARGIN) * 8, 128), F32),
            pltpu.VMEM((64, 128), I32),
            pltpu.SMEM((64, 128), I32),
            pltpu.SemaphoreType.DMA((5,)),
        ],
        compiler_params=pltpu.CompilerParams(vmem_limit_bytes=62 << 20),
        name="dispatch",
    )(patch.reshape(128, 128), span.reshape(128, 128), start, target)


def centre(c0, c1, c2, c3):
    outer, inner = c0 + c3, c1 + c2
    outer_diff, inner_diff = c3 - c0, c2 - c1
    return (0.125 * outer + 0.375 * inner, 0.75 * (outer_diff + inner_diff),
            1.5 * (outer - inner), outer_diff - 3.0 * inner_diff)


def value_slope(a, t):
    b2 = a[3] * t + a[2]
    b1 = b2 * t + a[1]
    return b1 * t + a[0], (a[3] * t + b2) * t + b1


def value_only(a, t):
    return ((a[3] * t + a[2]) * t + a[1]) * t + a[0]


def surface(load, u, v):
    u, v = u - 0.5, v - 0.5
    point, along_u, along_v = [], [], []
    for c in range(4):
        values, slopes = [], []
        for j in range(4):
            value, slope = value_slope([load(c * 16 + i * 4 + j) for i in range(4)], u)
            values.append(value)
            slopes.append(slope)
        h, hv = value_slope(values, v)
        point.append(h)
        along_u.append(value_only(slopes, v))
        along_v.append(hv)
    inverse = 1.0 / point[3]
    p = [point[c] * inverse for c in range(3)]
    su = [(along_u[c] - p[c] * along_u[3]) * inverse for c in range(3)]
    sv = [(along_v[c] - p[c] * along_v[3]) * inverse for c in range(3)]
    return p, su, sv


def dot3(a, b):
    return a[0] * b[0] + a[1] * b[1] + a[2] * b[2]


def project(load, goal, u, v, between):
    for _ in range(ITERS):
        p, su, sv = surface(load, u, v)
        miss = [p[c] - goal[c] for c in range(3)]
        gu, gv = dot3(su, miss), dot3(sv, miss)
        a, d, b = dot3(su, su) + DAMPING, dot3(sv, sv) + DAMPING, dot3(su, sv)
        inverse = 1.0 / (a * d - b * b)
        u, v = (jnp.clip(u - (d * gu - b * gv) * inverse, 0.0, 1.0),
                jnp.clip(v - (a * gv - b * gu) * inverse, 0.0, 1.0))
        between()
    return surface(load, u, v)


def project_kernel(out_ref, net_hbm, main_ref, last_ref,
                   net, recv, index_v, index_a, index_b, rows_a, rows_b, turned, control_a, control_b,
                   main, last, last_pair,
                   net_sem, index_sem, own, send, arrive, back, home):
    me = lax.axis_index("bulk")
    barrier = pltpu.get_barrier_semaphore()
    for k in range(1, OWNERS):
        peer = lax.rem(me + k, OWNERS)
        pl.semaphore_signal(barrier, inc=1, device_id={"bulk": peer}, device_id_type=MESH)
    def net_copy(k):
        return pltpu.make_async_copy(
            net_hbm.at[:, pl.ds(pl.multiple_of(k * 128, 128), 128)],
            net.at[pl.ds(pl.multiple_of(k * PITCH, 8), PATCH_DEV), :], net_sem.at[k])

    for k in range(8):
        net_copy(k).start()
    first = pltpu.make_async_copy(out_ref.at[me], recv.at[pl.ds(OWN * SLOT, SLOT), :], own.at[0])
    first.start()
    last[...] = jnp.zeros_like(last)
    pl.semaphore_wait(barrier, OWNERS - 1)

    def outward(k):
        peer = lax.rem(me + k, OWNERS)
        return pltpu.make_async_remote_copy(
            src_ref=out_ref.at[peer],
            dst_ref=recv.at[pl.ds(pl.multiple_of((k - 1) * SLOT, 8), SLOT), :],
            send_sem=send.at[k], recv_sem=arrive.at[k],
            device_id={"bulk": peer}, device_id_type=MESH,
        )

    def homeward(k, owner):
        peer = lax.rem(me + OWNERS - k, OWNERS)
        return [
            pltpu.make_async_remote_copy(
                src_ref=s.at[pl.ds(pl.multiple_of((k - 1) * n, 8), n), :],
                dst_ref=t.at[pl.ds(pl.multiple_of(owner * n, 8), n), :],
                send_sem=back.at[i, k], recv_sem=home.at[i, k],
                device_id={"bulk": peer}, device_id_type=MESH,
            )
            for i, (s, t, n) in enumerate(((main, main_ref, SLOT), (last, last_ref, 24)))
        ]

    stay = [
        pltpu.make_async_copy(main.at[pl.ds(OWN * SLOT, SLOT), :],
                              main_ref.at[pl.ds(pl.multiple_of(me * SLOT, 8), SLOT), :], own.at[1]),
        pltpu.make_async_copy(last.at[pl.ds(OWN * 24, 24), :],
                              last_ref.at[pl.ds(pl.multiple_of(me * 24, 8), 24), :], own.at[2]),
    ]

    def start_outward(k, carry):
        outward(k).start()
        return carry

    lax.fori_loop(1, OWNERS, start_outward, 0)

    def swap_halves(k, carry):
        net_copy(k).wait()
        for t in range(PITCH // 8):
            at = pl.multiple_of(k * PITCH + t * 8, 8)
            net[pl.ds(pl.multiple_of(at + TABLE, 8), 8), :] = pltpu.roll(net[pl.ds(at, 8), :], 64, axis=1)
        return carry

    lax.fori_loop(0, 8, swap_halves, 0)
    row, lane = iota((8, 128), 0), iota((8, 128), 1)
    masks = [[(row == s) & (lane < 64), (row == s) & (lane >= 64)] for s in range(8)]

    def prepare(m):
        for i in range(PAIR_BATCHES):
            b = m * PAIR_BATCHES + i
            code = recv[pl.ds(b * 64 + 5, 8, stride=8), :].astype(I32)
            code = jnp.clip(code, 0, 2 * TABLE - 1)
            swapped = jnp.where(code >= TABLE, code - TABLE, code + TABLE)
            index_v[b] = jnp.where((row & 1) == 1, swapped, code)

    def index_copy(b, half):
        return pltpu.make_async_copy(index_v.at[b], (index_a, index_b)[half], index_sem.at[half])

    def gather(index, rows, begin, end):
        for unit in range(begin, end):
            h, t = divmod(unit, 16)
            x = None
            for s in range(8):
                for q in range(2):
                    w = net[pl.ds(index[2 * h + q, t * 8 + s], 8, stride=0), :]
                    x = w if x is None else jnp.where(masks[s][q], w, x)
            rows[pl.ds(h * 128 + t * 8, 8), :] = x

    def to_powers(rows, control, between):
        for h in range(4):
            both = rows[pl.ds(h * 128, 128), :].T
            turned[pl.ds(2 * h * TURN, 64), :] = both[:64]
            turned[pl.ds((2 * h + 1) * TURN, 64), :] = both[64:]
            between()
        for c in range(4):
            along = [
                centre(*[turned[pl.ds(c * 16 + i * 4 + j, 8, stride=TURN), :] for i in range(4)])
                for j in range(4)
            ]
            for i in range(4):
                for j, x in enumerate(centre(*[along[j][i] for j in range(4)])):
                    control[c * 16 + i * 4 + j] = x
            between()

    first.wait()
    outward(1).wait_recv()
    outward(2).wait_recv()
    prepare(0)
    for half, (index, rows) in enumerate(((index_a, rows_a), (index_b, rows_b))):
        index_copy(half, half).start()
        index_copy(half, half).wait()
        gather(index, rows, 0, 64)
        index_copy(half + 2, half).start()
    to_powers(rows_a, control_a, lambda: None)

    def batch(b, half):
        index, rows, other, control, following = (
            (index_a, rows_a, rows_b, control_a, control_b),
            (index_b, rows_b, rows_a, control_b, control_a),
        )[half]
        m = lax.div(b, PAIR_BATCHES)
        i = b - m * PAIR_BATCHES
        index_copy(0, half).wait()
        cuts = iter(range(0, 64, FILL))

        def between():
            at = next(cuts, 64)
            gather(index, rows, at, min(at + FILL, 64))

        to_powers(other, following, between)

        def load(k):
            return control[k]

        def value(k):
            return recv[pl.ds(b * 64 + k, 8, stride=8), :]

        p, su, sv = project(load, [value(0), value(1), value(2)], value(3), value(4), between)
        for k, x in enumerate((p + su + sv)[:8]):
            main[pl.ds(b * 64 + k, 8, stride=8), :] = x
        last_pair[pl.ds(pl.multiple_of(i * 8, 8), 8), :] = sv[2]
        between()

        @pl.when((i == 1) & (m < OWNERS // 2 - 1))
        def _():
            outward(2 * m + 3).wait_recv()

            @pl.when(m < OWNERS // 2 - 2)
            def _():
                outward(2 * m + 4).wait_recv()

            prepare(m + 1)

        index_copy(jnp.minimum(b + 4, BATCHES - 1), half).start()

        def keep_last(h):
            at = pl.multiple_of((2 * m + h) * 24, 8)
            last[pl.ds(at, TILES), :] = last_pair[h * TILES:(h + 1) * TILES, :]

        @pl.when(i == 2)
        def _():
            keep_last(0)
            for copy in homeward(2 * m + 1, me):
                copy.start()

        @pl.when(i == PAIR_BATCHES - 1)
        def _():
            keep_last(1)

            @pl.when(m < OWNERS // 2 - 1)
            def _():
                for copy in homeward(2 * m + 2, me):
                    copy.start()

            @pl.when(m == OWNERS // 2 - 1)
            def _():
                for copy in stay:
                    copy.start()

    def two(q, carry):
        batch(2 * q, 0)
        batch(2 * q + 1, 1)
        return carry

    lax.fori_loop(0, BATCHES // 2, two, 0)
    for half in range(2):
        index_copy(0, half).wait()
    for copy in stay:
        copy.wait()

    def finish(k, carry):
        outward(k).wait_send()
        for copy in homeward(k, lax.rem(me + k, OWNERS)):
            copy.wait()
        return carry

    lax.fori_loop(1, OWNERS, finish, 0)


def place_nodes(outgoing, net):
    vmem = pl.BlockSpec(memory_space=pltpu.VMEM)
    dma = pltpu.SemaphoreType.DMA
    return pl.pallas_call(
        project_kernel,
        out_shape=[
            jax.ShapeDtypeStruct((GROUPS * 8 + 24, 128), F32),
            jax.ShapeDtypeStruct((OWNERS * 24, 128), F32),
        ],
        in_specs=[pl.BlockSpec(memory_space=pltpu.HBM), pl.BlockSpec(memory_space=pl.ANY)],
        out_specs=[vmem] * 2,
        scratch_shapes=[
            pltpu.VMEM((2 * TABLE, 128), F32),
            pltpu.VMEM((GROUPS * 8 + 64, 128), F32),
            pltpu.VMEM((BATCHES, 8, 128), I32),
            pltpu.SMEM((8, 128), I32),
            pltpu.SMEM((8, 128), I32),
            pltpu.VMEM((BATCH * 64, 128), F32),
            pltpu.VMEM((BATCH * 64, 128), F32),
            pltpu.VMEM((BATCH * TURN + 64, 128), F32),
            pltpu.VMEM((64, 8, 128), F32),
            pltpu.VMEM((64, 8, 128), F32),
            pltpu.VMEM((GROUPS * 8 + 64, 128), F32),
            pltpu.VMEM((OWNERS * 24, 128), F32),
            pltpu.VMEM((2 * TILES, 128), F32),
            dma((8,)), dma((2,)), dma((3,)),
            dma((OWNERS,)), dma((OWNERS,)), dma((2, OWNERS)), dma((2, OWNERS)),
        ],
        compiler_params=pltpu.CompilerParams(
            collective_id=1, has_side_effects=True, vmem_limit_bytes=48 << 20),
        name="project",
    )(outgoing, net)


def collect_kernel(main, last, place_ref, table_hbm, out_ref, ordered, table_s, sem):
    copy = pltpu.make_async_copy(table_hbm, table_s, sem)
    copy.start()
    copy.wait()
    lane = iota((8, 128), 1)

    def assemble(j):
        acc = [jnp.zeros((8, 128), F32) for _ in range(4)]
        for o in range(OWNERS):
            move, offset = table_s[j, o], table_s[j, 16 + o]
            tile, first = table_s[j, 32 + o], table_s[j, 64 + o]
            at = pl.multiple_of((o * TILES + tile) * 8, 8)
            at_last = o * 24 + tile
            keep = lane >= offset
            in_low, in_high = lane >= first, lane >= first - 128
            from_low = lane >= 128 - move
            from_high = (lane >= -move) & (lane < 128 - move)
            windows = (
                [main[pl.ds(at + 8 * k, 8), :] for k in range(3)],
                [last[pl.ds(at_last + k, 8, stride=0), :] for k in range(3)],
            )
            for k, (w0, w1, w2) in enumerate(windows):
                r0 = pltpu.roll(jnp.where(keep, w0, w2), (-move) & 127, axis=1)
                r1 = pltpu.roll(w1, (-move) & 127, axis=1)
                acc[2 * k] = jnp.where(in_low, jnp.where(from_low, r1, r0), acc[2 * k])
                acc[2 * k + 1] = jnp.where(in_high, jnp.where(from_high, r1, r0), acc[2 * k + 1])
        return acc

    def keep_block(j, acc):
        for k in range(2):
            ordered[j, 8 * k:8 * k + 8, 0:128] = acc[2 * k]
            ordered[j, 8 * k:8 * k + 8, 128:256] = acc[2 * k + 1]

    for step in range(STEPS):
        keep_block(step, assemble(step))

    def spread(i, carry):
        ready = [ordered[i * STEPS + step] for step in range(STEPS)]
        for step in range(STEPS):
            j = i * STEPS + step
            y = jnp.dot(split3(ready[step]), block_permutation(place_ref, j), preferred_element_type=F32)
            y = y[0:16] + y[16:32] + y[32:48]
            for h in range(2):
                at = pl.multiple_of((j + 64 * h) * 128, 128)
                out_ref[:, pl.ds(at, 128)] = y[0:9, h * 128:(h + 1) * 128]
            coming = jnp.minimum((i + 1) * STEPS, 64 - STEPS) + step
            keep_block(coming, assemble(coming))
        return carry

    lax.fori_loop(0, 64 // STEPS, spread, 0)


def collect(main, last, place, table):
    vmem = pl.BlockSpec(memory_space=pltpu.VMEM)
    hbm = pl.BlockSpec(memory_space=pl.ANY)
    return pl.pallas_call(
        collect_kernel,
        out_shape=jax.ShapeDtypeStruct((9, 16384), F32),
        in_specs=[vmem, vmem, vmem, hbm],
        out_specs=vmem,
        scratch_shapes=[pltpu.VMEM((64, 16, 256), F32), pltpu.SMEM((64, 128), I32), pltpu.SemaphoreType.DMA],
        compiler_params=pltpu.CompilerParams(vmem_limit_bytes=32 << 20),
        name="collect",
    )(main, last, place, table)


def body(node_patch, node_span, start_grid, target, net):
    outgoing, place, table = dispatch(node_patch, node_span, start_grid, target)
    outgoing = pltpu.with_memory_space_constraint(outgoing, pltpu.HBM)
    main, last = place_nodes(outgoing, net)
    return collect(main, last, place, table)


def solution(mesh):
    return jax.shard_map(
        body,
        mesh=mesh,
        in_specs=(
            P(("dom", "bulk")),
            P(("dom", "bulk")),
            P(None, ("dom", "bulk")),
            P(None, ("dom", "bulk")),
            P("bulk", None),
        ),
        out_specs=P(None, ("dom", "bulk")),
        check_vma=False,
    )
```
